32 devices in a mesh: row: 4 (over x, core), col: 8 (over z, y).
Axes of the slice: x: 2, y: 2, z: 4, core: 2. Of those that a mesh axis runs over, the one named last changes fastest.
Arguments:
- pair: bfloat16 [768, 768, 512], P('row', 'col'), may hold values from -6 to 6
- w_bias: bfloat16 [512, 96], replicated, may hold values from -0.25 to 0.25
- queries: bfloat16 [768, 1536], P('row', 'col'), may hold values from -360 to 360
- keys: bfloat16 [768, 1536], P('col', 'row'), may hold values from -6 to 6
- values: bfloat16 [768, 1536], P('col', 'row'), may hold values from -6 to 6
- d_out: bfloat16 [768, 1536], P('row', 'col'), may hold values from -6 to 6
Outputs:
- d_pair: bfloat16 [768, 768, 512], P('row', 'col')
- d_wbias: float32 [512, 96], replicated
- d_queries: bfloat16 [768, 1536], P('row', 'col')
- d_keys: bfloat16 [768, 1536], P('col', 'row')
- d_values: bfloat16 [768, 1536], P('col', 'row')
The draws below stay inside these ranges and needn't reach their ends.
All inputs are finite; a program needn't handle non-finite values.
Results may differ from the reference program's by a relative error of at most 0.0095.
Values may be sent and summed in bfloat16 or wider, within the bound.
A program may use at most 128 MiB of HBM per device.

```python
import jax
import jax.numpy as jnp
from jax import lax

D = 1536
H = 96
P_SIZE = 512
N = 768
HD = 16


def draw_entries(key):
    base = jax.random.fold_in(key, 7101)
    query_key, key_key = jax.random.split(base, 2)
    query_draw = jnp.clip(jax.random.normal(query_key, (N, D), jnp.float32), -6.0, 6.0)
    key_draw = jnp.clip(jax.random.normal(key_key, (N, D), jnp.float32), -6.0, 6.0)
    return (query_draw, key_draw)


def draw_queries(key, part):
    return draw_entries(key)[0].astype(jnp.bfloat16)


def draw_keys(key, part):
    return draw_entries(key)[1].astype(jnp.bfloat16)


def block_scale(own_key, extent, cuts, least, largest):
    loudness, own = 1.0, jax.random.fold_in(own_key, 6)
    for axis_at, parts in cuts:
        heights = jnp.exp(jax.random.uniform(jax.random.fold_in(own, axis_at), (parts,), jnp.float32, least / len(cuts), largest / len(cuts)))
        loudness = loudness * jnp.repeat(heights, extent[axis_at] // parts).reshape([-1 if axis == axis_at else 1 for axis in range(len(extent))])
    return loudness


def scatter_about(key, dims, scale, limit, shards=(), held_as=jnp.bfloat16):
    gain = block_scale(key, dims, shards, -0.22, 0.18) if shards else 1.0
    drawn = jax.random.normal(key, dims, jnp.float32) * scale * gain
    return jnp.minimum(jnp.maximum(drawn, -limit), limit).astype(held_as)


def setup_inputs(seed: int = 0) -> dict:
    key_of = jax.random.split(jax.random.key(seed), 7)
    return {
        "pair": scatter_about(key_of[0], (N, N, P_SIZE), 1.0, 6.0, ((0, 4), (1, 8))),
        "w_bias": scatter_about(key_of[1], (P_SIZE, H), P_SIZE ** -0.5, 0.25),
        "queries": draw_queries(jax.random.fold_in(key_of[6], 71), 0),
        "keys": draw_keys(jax.random.fold_in(key_of[6], 71), 0),
        "values": scatter_about(key_of[4], (N, D), 1.0, 6.0, ((0, 8), (1, 4))),
        "d_out": scatter_about(key_of[5], (N, D), 1.0, 6.0, ((0, 4), (1, 8))),
    }


def reference(pair, w_bias, queries, keys, values, d_out):
    block_rows = N // 16
    scale = 1.0 / (HD ** 0.5)
    key_heads = keys.astype(jnp.float32).reshape(N, H, HD)
    value_heads = values.astype(jnp.float32).reshape(N, H, HD)

    def advance(totals, block_index):
        grad_keys, grad_values, grad_weight = totals
        offset = (block_index * block_rows).astype(jnp.int32)
        pair_block = lax.dynamic_slice_in_dim(pair, offset, block_rows, 0)
        query_heads = lax.dynamic_slice_in_dim(queries, offset, block_rows, 0).astype(jnp.float32).reshape(block_rows, H, HD)
        out_heads = lax.dynamic_slice_in_dim(d_out, offset, block_rows, 0).astype(jnp.float32).reshape(block_rows, H, HD)
        flat_pair = pair_block.reshape(block_rows * N, P_SIZE)
        pair_bias = jnp.dot(flat_pair, w_bias, preferred_element_type=jnp.float32).reshape(block_rows, N, H)
        scores = jnp.einsum('ihd,jhd->hij', query_heads, key_heads) * scale + pair_bias.transpose(2, 0, 1)
        weights = jax.nn.softmax(scores, axis=-1)
        grad_prob = jnp.einsum('ihd,jhd->hij', out_heads, value_heads)
        row_delta = jnp.sum(weights * grad_prob, axis=-1, keepdims=True)
        grad_score = (weights * (grad_prob - row_delta)).astype(jnp.bfloat16)
        weights_low = weights.astype(jnp.bfloat16)
        score_flat = grad_score.transpose(1, 2, 0).reshape(block_rows * N, H)
        pair_grad = jnp.dot(score_flat, w_bias.T, preferred_element_type=jnp.float32).astype(jnp.bfloat16).reshape(block_rows, N, P_SIZE)
        grad_weight = grad_weight + jnp.dot(flat_pair.T, score_flat, preferred_element_type=jnp.float32)
        score_wide = grad_score.astype(jnp.float32)
        query_grad = (jnp.einsum('hij,jhd->ihd', score_wide, key_heads) * scale).reshape(block_rows, D).astype(jnp.bfloat16)
        grad_keys = grad_keys + (jnp.einsum('hij,ihd->jhd', score_wide, query_heads) * scale).reshape(N, D)
        grad_values = grad_values + jnp.einsum('hij,ihd->jhd', weights_low.astype(jnp.float32), out_heads).reshape(N, D)
        return (grad_keys, grad_values, grad_weight), (pair_grad, query_grad)

    start_totals = (jnp.zeros((N, D), jnp.float32), jnp.zeros((N, D), jnp.float32), jnp.zeros((P_SIZE, H), jnp.float32))
    totals, pieces = lax.scan(advance, start_totals, jnp.arange(16, dtype=jnp.int32))
    d_pair = pieces[0].reshape(N, N, P_SIZE)
    d_queries = pieces[1].reshape(N, D)
    return d_pair, totals[2], d_queries, totals[0].astype(jnp.bfloat16), totals[1].astype(jnp.bfloat16)
```

```python
import functools

import jax
import jax.numpy as jnp
from jax import lax
from jax.experimental import pallas as pl
from jax.experimental.pallas import tpu as pltpu
from jax.sharding import PartitionSpec as P

HD = 16
SCALE = 1.0 / HD**0.5
LANES = 128
STEP = 16
SLOTS = 2
MESH = pl.DeviceIdType.MESH
VMEM = pltpu.VMEM
DMA = pltpu.SemaphoreType.DMA
F32 = jnp.float32
BF16 = jnp.bfloat16


def remote(src, dst, send, recv, row, col):
    return pltpu.make_async_remote_copy(
        src_ref=src, dst_ref=dst, send_sem=send, recv_sem=recv,
        device_id=(row, col), device_id_type=MESH,
    )


def greet(nrow, ncol, row, col):
    barrier = pltpu.get_barrier_semaphore()
    for k in range(1, ncol):
        pl.semaphore_signal(
            barrier, inc=1, device_id=(row, lax.rem(col + k, ncol)), device_id_type=MESH
        )
    for k in range(1, nrow):
        pl.semaphore_signal(
            barrier, inc=1, device_id=(lax.rem(row + k, nrow), col), device_id_type=MESH
        )
    pl.semaphore_wait(barrier, ncol + nrow - 2)


def dot(a, b):
    return jnp.dot(a, b, preferred_element_type=F32)


def dot_nt(a, b):
    return lax.dot_general(a, b, (((1,), (1,)), ((), ())), preferred_element_type=F32)


def main_kernel(
    nrow, ncol, wt, pair, q, k_in, v, d,
    f_out, wb_out, q_out, k_out, v_out,
    pv, bias, e_buf, g_buf, qd, kv, qd_all, kv_all, qt, dt, kt, vt,
    st, got, back, bk, dq, dq_got, dkv, dkv_got,
    acc, wb, w1, w1sum, w2, w2sum, f_st,
    psem, qs, qr, fs, fr, ks, kr, s1, r1, s2, r2, gs, gr, hs, hr_sem,
    ws1, wr1, ws2, wr2, ws3, wr3, ws4, wr4, fsem,
):
    row, col = lax.axis_index("row"), lax.axis_index("col")
    R, C, W = pair.shape
    H = wt.shape[0]
    Cp = pv.shape[1]
    hb, hr = H // ncol, H // nrow
    dcol, drow = hb * HD, hr * HD
    wr = W // nrow
    chunks = R // STEP
    inner = 2 if ncol % 2 == 0 else 1
    outer = ncol // inner
    a, b_in = col // inner, lax.rem(col, inner)
    flip = a * inner + inner - 1 - b_in

    def load(t):
        rows = pl.ds(t * STEP, STEP)
        return pltpu.make_async_copy(pair.at[rows], pv.at[rows, pl.ds(0, C)], psem.at[t])

    @pl.loop(0, chunks)
    def _(t):
        load(t).start()

    qd_own = jnp.concatenate([q[...], d[...]], axis=1)
    kv_own = jnp.concatenate([k_in[...], v[...]], axis=1)
    qd[...] = qd_own
    kv[...] = kv_own
    qd_all[col] = qd_own
    kv_all[row] = kv_own
    greet(nrow, ncol, row, col)

    def relay(k):
        src = lax.rem(a + outer - k, outer) * inner + b_in
        return remote(qd_all.at[src], qd_all.at[src], fs.at[k], fr.at[k], row, flip)

    first = []
    for k in range(1, outer):
        to = lax.rem(a + k, outer) * inner + b_in
        first.append(remote(qd, qd_all.at[col], qs.at[k], qr.at[k], row, to))
    if inner == 2:
        first.append(remote(qd, qd_all.at[col], fs.at[0], fr.at[0], row, flip))
    for k in range(1, nrow):
        to = lax.rem(row + k, nrow)
        first.append(remote(kv, kv_all.at[row], ks.at[k], kr.at[k], to, col))
    for copy in first:
        copy.start()
    if Cp > C:
        pv[:, C:, :] = jnp.zeros((R, Cp - C, W), BF16)

    @pl.loop(0, chunks)
    def _(t):
        load(t).wait()
        for u in range(0, STEP, 2):
            i = t * STEP + u
            r = dot_nt(wt[...], pv[pl.ds(i, 2)].reshape(2 * Cp, W))
            bias[pl.ds(i, H, stride=R), :] = r[:, :Cp]
            bias[pl.ds(i + 1, H, stride=R), :] = r[:, Cp:]
        for k in range(1, outer):

            @pl.when(t == min(chunks - 1, chunks // 2 + 2 * (k - 1)))
            def _():
                src = lax.rem(a + outer - k, outer) * inner + b_in
                remote(qd, qd_all.at[src], qs.at[k], qr.at[k], row, col).wait_recv()
                if inner == 2:
                    relay(k).start()

    for k in range(1, nrow):
        src = lax.rem(row + nrow - k, nrow)
        remote(kv, kv_all.at[src], ks.at[k], kr.at[k], row, col).wait_recv()

    @pl.loop(0, nrow)
    def _(r):
        x = kv_all[r].T
        kt[pl.ds(r * hr, hr)] = x[:drow].reshape(hr, HD, C)
        vt[pl.ds(r * hr, hr)] = x[drow:].reshape(hr, HD, C)

    if inner == 2:
        for k in range(outer):
            src = lax.rem(a + outer - k, outer) * inner + 1 - b_in
            remote(qd, qd_all.at[src], fs.at[k], fr.at[k], row, col).wait_recv()

    lag = ncol // 2

    def combine():
        for k in range(1, ncol):
            src = lax.rem(col + k, ncol)
            remote(st.at[src], got.at[src], s1.at[src], r1.at[src], row, col).wait_recv()
        got[col] = st[col]
        top = got[0, 0]
        for k in range(1, ncol):
            top = jnp.maximum(top, got[k, 0])
        total = jnp.zeros_like(top)
        upper = jnp.zeros_like(top)
        for k in range(ncol):
            scale = jnp.exp(got[k, 0] - top)
            total += got[k, 1] * scale
            upper += got[k, 2] * scale
        delta = upper / total
        for k in range(ncol):
            back[k, 0] = jnp.exp(got[k, 0] - top) / total
            back[k, 1] = delta
        bk[col] = back[col]
        for k in range(1, ncol):
            to = lax.rem(col + k, ncol)
            remote(back.at[to], bk.at[col], s2.at[to], r2.at[col], row, to).start()

    @pl.loop(0, ncol)
    def _(b):
        x = qd_all[b].T
        qt[pl.ds(b * hb, hb)] = (x[:dcol] * jnp.asarray(SCALE, BF16)).reshape(hb, HD, R)
        dt[pl.ds(b * hb, hb)] = x[dcol:].reshape(hb, HD, R)
        heads = pl.ds(b * hb, hb)
        kb = kt[heads].reshape(dcol, C).T
        vb = vt[heads].reshape(dcol, C).T
        qb = qt[heads].reshape(dcol, R)
        db = dt[heads].reshape(dcol, R)
        owner = lax.broadcasted_iota(jnp.int32, (C, dcol), 1) // HD
        zero = jnp.zeros((C, dcol), BF16)
        for t in range(hb):
            h = b * hb + t
            term = bias[pl.ds(pl.multiple_of(h * R, 8), R), :].T[:C]
            s = dot(jnp.where(owner == t, kb, zero), qb) + term
            g = dot(jnp.where(owner == t, vb, zero), db)
            top = jnp.max(s, axis=0, keepdims=True)
            e = jnp.exp(s - top)
            e_buf[h] = e
            g_buf[h] = g
            st[b, 0, pl.ds(t, 1)] = top
            st[b, 1, pl.ds(t, 1)] = jnp.sum(e, axis=0, keepdims=True)
            st[b, 2, pl.ds(t, 1)] = jnp.sum(e * g, axis=0, keepdims=True)

        @pl.when(col != b)
        def _():
            remote(st.at[b], got.at[col], s1.at[b], r1.at[col], row, b).start()

        @pl.when(col == b - lag)
        def _():
            combine()

    per = hr // hb if hr % hb == 0 else 0

    def send_dkv(r):
        remote(dkv.at[r], dkv_got.at[row], gs.at[r], gr.at[row], r, col).start()

    @pl.loop(0, ncol)
    def _(b):
        @pl.when(col == ncol - lag + b)
        def _():
            combine()

        @pl.when(col != b)
        def _():
            remote(back.at[b], bk.at[b], s2.at[b], r2.at[b], row, col).wait_recv()

        for t in range(hb):
            h = b * hb + t
            r = h // hr
            w = e_buf[h] * bk[b, 0, pl.ds(t, 1)]
            ds = (w * (g_buf[h] - bk[b, 1, pl.ds(t, 1)])).astype(BF16)
            low = w.astype(BF16)
            dq[b, t] = (dot(kt[h], ds) * SCALE).astype(BF16)
            dkv[r, 0, lax.rem(h, hr)] = dot_nt(qt[h], ds).astype(BF16)
            dkv[r, 1, lax.rem(h, hr)] = dot_nt(dt[h], low).astype(BF16)
            bias[pl.ds(pl.multiple_of(h * R, 8), R), pl.ds(0, C)] = ds.astype(F32).T

        @pl.when(col != b)
        def _():
            remote(dq.at[b], dq_got.at[col], hs.at[b], hr_sem.at[col], row, b).start()

        if per:
            done = b // per

            @pl.when(jnp.logical_and(lax.rem(b, per) == per - 1, row != done))
            def _():
                send_dkv(done)

    if not per:
        for k in range(1, nrow):
            send_dkv(lax.rem(row + k, nrow))

    acc[...] = jnp.zeros_like(acc)

    def rows_of(i):
        return bias[pl.ds(i, H, stride=R), :]

    @pl.loop(0, chunks)
    def _(t):
        total = acc[...]
        for u in range(0, STEP, 2):
            i = t * STEP + u
            lhs = jnp.concatenate(
                [rows_of(i).astype(BF16), rows_of(i + 1).astype(BF16)], axis=1
            )
            total = total + dot(lhs, pv[pl.ds(i, 2)].reshape(2 * Cp, W))
        acc[...] = total

    for r in range(nrow):
        for b in range(ncol):
            wb[r, b] = acc[b * hb:(b + 1) * hb, r * wr:(r + 1) * wr]

    def put(t, slot):
        return pltpu.make_async_copy(
            f_st.at[slot], f_out.at[pl.ds(t * STEP, STEP)], fsem.at[slot]
        )

    def flat(lo, hi):
        @pl.loop(lo, hi)
        def _(t):
            slot = lax.rem(t, SLOTS)

            @pl.when(t >= SLOTS)
            def _():
                put(t - SLOTS, slot).wait()

            for u in range(STEP):
                f_st[slot, u] = rows_of(t * STEP + u).T[:C].astype(BF16)
            put(t, slot).start()

    cuts = [0, chunks // 4, (2 * chunks) // 3, chunks - chunks // 8, chunks]

    for k in range(1, nrow):
        to = lax.rem(row + k, nrow)
        remote(wb.at[to], w1.at[k], ws1.at[k], wr1.at[k], to, col).start()
    flat(cuts[0], cuts[1])
    total = wb[row]
    for k in range(1, nrow):
        remote(wb.at[0], w1.at[k], ws1.at[k], wr1.at[k], row, col).wait_recv()
        total += w1[k]
    w1sum[...] = total
    for k in range(1, ncol):
        to = lax.rem(col + k, ncol)
        remote(w1sum.at[to], w2.at[k], ws2.at[k], wr2.at[k], row, to).start()
    flat(cuts[1], cuts[2])
    part = w1sum[col]
    for k in range(1, ncol):
        remote(w1sum.at[0], w2.at[k], ws2.at[k], wr2.at[k], row, col).wait_recv()
        part += w2[k]
    w2sum[...] = part
    wb_out[row, col] = part
    for k in range(1, ncol):
        to = lax.rem(col + k, ncol)
        remote(w2sum, wb_out.at[row, col], ws3.at[k], wr3.at[k], row, to).start()
    flat(cuts[2], cuts[3])

    grad = dkv[row].astype(F32)
    for k in range(1, nrow):
        src = lax.rem(row + k, nrow)
        remote(dkv.at[0], dkv_got.at[src], gs.at[0], gr.at[src], row, col).wait_recv()
        grad += dkv_got[src].astype(F32)
    k_out[...] = grad[0].reshape(drow, C).T.astype(BF16)
    v_out[...] = grad[1].reshape(drow, C).T.astype(BF16)
    total_q = dq[col].astype(F32)
    for k in range(1, ncol):
        src = lax.rem(col + k, ncol)
        remote(dq.at[0], dq_got.at[src], hs.at[0], hr_sem.at[src], row, col).wait_recv()
        total_q += dq_got[src].astype(F32)
    q_out[...] = total_q.reshape(dcol, R).T.astype(BF16)

    for k in range(1, ncol):
        src = lax.rem(col + ncol - k, ncol)
        remote(w2sum, wb_out.at[row, src], ws3.at[k], wr3.at[k], row, col).wait_recv()
    for k in range(1, nrow):
        to = lax.rem(row + k, nrow)
        remote(wb_out.at[row], wb_out.at[row], ws4.at[k], wr4.at[k], to, col).start()
    flat(cuts[3], cuts[4])
    for k in range(1, nrow):
        src = lax.rem(row + nrow - k, nrow)
        remote(wb_out.at[src], wb_out.at[src], ws4.at[k], wr4.at[k], row, col).wait_recv()

    for t in range(max(0, chunks - SLOTS), chunks):
        put(t, t % SLOTS).wait()
    for copy in first:
        copy.wait_send()
    if inner == 2:
        for k in range(1, outer):
            relay(k).wait_send()
    for k in range(1, ncol):
        to = lax.rem(col + k, ncol)
        remote(st.at[to], got.at[col], s1.at[to], r1.at[col], row, to).wait_send()
        remote(back.at[to], bk.at[col], s2.at[to], r2.at[col], row, to).wait_send()
        remote(dq.at[to], dq_got.at[col], hs.at[to], hr_sem.at[col], row, to).wait_send()
        remote(w1sum.at[to], w2.at[k], ws2.at[k], wr2.at[k], row, to).wait_send()
        remote(w2sum, wb_out.at[row, col], ws3.at[k], wr3.at[k], row, to).wait_send()
    for k in range(1, nrow):
        to = lax.rem(row + k, nrow)
        remote(dkv.at[to], dkv_got.at[row], gs.at[to], gr.at[row], to, col).wait_send()
        remote(wb.at[to], w1.at[k], ws1.at[k], wr1.at[k], to, col).wait_send()
        remote(wb_out.at[row], wb_out.at[row], ws4.at[k], wr4.at[k], to, col).wait_send()


def main(nrow, ncol, wt, pair, q, k, v, d):
    R, C, W = pair.shape
    H = wt.shape[0]
    hb, hr = H // ncol, H // nrow
    dcol, drow = q.shape[1], k.shape[1]
    Cp = -(-C // LANES) * LANES
    wr = W // nrow
    shape = jax.ShapeDtypeStruct
    return pl.pallas_call(
        functools.partial(main_kernel, nrow, ncol),
        out_shape=(
            shape((R, C, H), BF16),
            shape((nrow, ncol, hb, wr), F32),
            shape((R, dcol), BF16),
            shape((C, drow), BF16),
            shape((C, drow), BF16),
        ),
        in_specs=[pl.BlockSpec(memory_space=VMEM), pl.BlockSpec(memory_space=pl.ANY)]
        + [pl.BlockSpec(memory_space=VMEM)] * 4,
        out_specs=[pl.BlockSpec(memory_space=pl.ANY)] + [pl.BlockSpec(memory_space=VMEM)] * 4,
        scratch_shapes=[
            VMEM((R, Cp, W), BF16),
            VMEM((H * R, Cp), F32),
            VMEM((H, C, R), F32),
            VMEM((H, C, R), F32),
            VMEM((R, 2 * dcol), BF16),
            VMEM((C, 2 * drow), BF16),
            VMEM((ncol, R, 2 * dcol), BF16),
            VMEM((nrow, C, 2 * drow), BF16),
            VMEM((H, HD, R), BF16),
            VMEM((H, HD, R), BF16),
            VMEM((H, HD, C), BF16),
            VMEM((H, HD, C), BF16),
            VMEM((ncol, 3, hb, R), F32),
            VMEM((ncol, 3, hb, R), F32),
            VMEM((ncol, 2, hb, R), F32),
            VMEM((ncol, 2, hb, R), F32),
            VMEM((ncol, hb, HD, R), BF16),
            VMEM((ncol, hb, HD, R), BF16),
            VMEM((nrow, 2, hr, HD, C), BF16),
            VMEM((nrow, 2, hr, HD, C), BF16),
            VMEM((H, W), F32),
            VMEM((nrow, ncol, hb, wr), F32),
            VMEM((nrow, ncol, hb, wr), F32),
            VMEM((ncol, hb, wr), F32),
            VMEM((ncol, hb, wr), F32),
            VMEM((hb, wr), F32),
            VMEM((SLOTS, STEP, C, H), BF16),
            DMA((R // STEP,)),
            DMA((ncol,)), DMA((ncol,)), DMA((ncol,)), DMA((ncol,)),
            DMA((nrow,)), DMA((nrow,)),
            DMA((ncol,)), DMA((ncol,)), DMA((ncol,)), DMA((ncol,)),
            DMA((nrow,)), DMA((nrow,)), DMA((ncol,)), DMA((ncol,)),
            DMA((nrow,)), DMA((nrow,)), DMA((ncol,)), DMA((ncol,)),
            DMA((ncol,)), DMA((ncol,)), DMA((nrow,)), DMA((nrow,)),
            DMA((SLOTS,)),
        ],
        compiler_params=pltpu.CompilerParams(
            collective_id=0, has_side_effects=True, vmem_limit_bytes=67043328
        ),
    )(wt, pair, q, k, v, d)


def finish_kernel(f, wt, wb, q, k, v, d_pair, wo, qo, ko, vo):
    rows, C, H = f.shape
    d_pair[...] = dot(f[...].reshape(rows * C, H), wt[...]).astype(BF16).reshape(d_pair.shape)

    @pl.when(pl.program_id(0) == 0)
    def _():
        qo[...] = q[...]
        ko[...] = k[...]
        vo[...] = v[...]
        nrow, wr = wb.shape[0], wb.shape[3]
        for r in range(nrow):
            wo[:, r * wr:(r + 1) * wr] = wb[r].reshape(H, wr)


def finish(f, wt, wb, q, k, v, block=16):
    R, C, H = f.shape
    W = wt.shape[1]

    def whole(x):
        return pl.BlockSpec(x.shape, lambda i: (0,) * len(x.shape))

    return pl.pallas_call(
        finish_kernel,
        grid=(R // block,),
        out_shape=(
            jax.ShapeDtypeStruct((R, C, W), BF16),
            jax.ShapeDtypeStruct((H, W), F32),
            jax.ShapeDtypeStruct(q.shape, BF16),
            jax.ShapeDtypeStruct(k.shape, BF16),
            jax.ShapeDtypeStruct(v.shape, BF16),
        ),
        in_specs=[pl.BlockSpec((block, C, H), lambda i: (i, 0, 0))]
        + [whole(x) for x in (wt, wb, q, k, v)],
        out_specs=(
            pl.BlockSpec((block, C, W), lambda i: (i, 0, 0)),
            pl.BlockSpec((H, W), lambda i: (0, 0)),
            whole(q), whole(k), whole(v),
        ),
    )(f, wt, wb, q, k, v)


def on_device(nrow, ncol, pair, w_bias, queries, keys, values, d_out):
    wt = w_bias.T
    f, wb, q, k, v = main(nrow, ncol, wt, pair, queries, keys, values, d_out)
    d_pair, d_wbias, d_queries, d_keys, d_values = finish(f, wt, wb, q, k, v)
    return d_pair, d_wbias.T, d_queries, d_keys, d_values


def solution(mesh):
    return jax.shard_map(
        functools.partial(on_device, mesh.shape["row"], mesh.shape["col"]),
        mesh=mesh,
        in_specs=(
            P("row", "col", None),
            P(),
            P("row", "col"),
            P("col", "row"),
            P("col", "row"),
            P("row", "col"),
        ),
        out_specs=(P("row", "col", None), P(), P("row", "col"), P("col", "row"), P("col", "row")),
        check_vma=False,
    )
```

```python
import functools

import jax
import jax.numpy as jnp
from jax import lax
from jax.experimental import pallas as pl
from jax.experimental.pallas import tpu as pltpu
from jax.sharding import PartitionSpec as P

HD = 16
SCALE = 1.0 / HD**0.5
LANES = 128
STEP = 16
SLOTS = 2
HOP = 4
MESH = pl.DeviceIdType.MESH
VMEM = pltpu.VMEM
DMA = pltpu.SemaphoreType.DMA
F32 = jnp.float32
BF16 = jnp.bfloat16


def remote(src, dst, send, recv, row, col):
    return pltpu.make_async_remote_copy(
        src_ref=src, dst_ref=dst, send_sem=send, recv_sem=recv,
        device_id=(row, col), device_id_type=MESH,
    )


def split(n):
    return (2, n // 2) if n % 2 == 0 else (1, n)


def folds(R, hb):
    half = R % LANES
    return R == LANES + half and 2 * half == LANES and hb % 2 == 0, half


def greet(nrow, ncol, row, col):
    barrier = pltpu.get_barrier_semaphore()
    for k in range(1, ncol):
        pl.semaphore_signal(
            barrier, inc=1, device_id=(row, lax.rem(col + k, ncol)), device_id_type=MESH
        )
    for k in range(1, nrow):
        pl.semaphore_signal(
            barrier, inc=1, device_id=(lax.rem(row + k, nrow), col), device_id_type=MESH
        )
    pl.semaphore_wait(barrier, ncol + nrow - 2)


def dot(a, b):
    return jnp.dot(a, b, preferred_element_type=F32)


def dot_nt(a, b):
    return lax.dot_general(a, b, (((1,), (1,)), ((), ())), preferred_element_type=F32)


def main_kernel(
    nrow, ncol, wt, pair, q, k_in, v, d,
    f_out, wb_out, q_out, k_out, v_out,
    pv, bias, e_buf, g_buf, qd, kv, qd_all, kv_all, qt, dt, kt, vt,
    st, got, back, bk, dq, dq_near, dq_far, dkv, dkv_near, dkv_far,
    acc, wb, w1, w1sum, w2, w2sum, f_st,
    psem, up_s, down_s, zr, fs, fr, ks, kr, js, jr, s1, r1, s2, r2,
    qn_s, qn_r, qf_s, qf_r, gn_s, gn_r, gf_s, gf_r,
    ws1, wr1, ws2, wr2, ws3, wr3, ws4, wr4, fsem,
):
    row, col = lax.axis_index("row"), lax.axis_index("col")
    R, C, W = pair.shape
    H = wt.shape[0]
    Cp = pv.shape[1]
    hb, hr = H // ncol, H // nrow
    dcol, drow = hb * HD, hr * HD
    wr = W // nrow
    chunks = R // STEP
    inner, outer, rin, rout = split(ncol) + split(nrow)
    a, b_in = col // inner, lax.rem(col, inner)
    flip = a * inner + inner - 1 - b_in
    x_at, core = row // rin, lax.rem(row, rin)
    twin = x_at * rin + rin - 1 - core
    folded, half = folds(R, hb)
    main_lanes = LANES if folded else R

    def put_row(ref, b, s, n, x):
        ref[b, s:s + 1, :] = x[:, :main_lanes]
        if folded:
            at = (s % 2) * half
            ref[b, n + s // 2:n + s // 2 + 1, at:at + half] = x[:, main_lanes:]

    def get_row(ref, b, s, n):
        x = ref[b, s:s + 1, :]
        if folded:
            at = (s % 2) * half
            tail = ref[b, n + s // 2:n + s // 2 + 1, at:at + half]
            x = jnp.concatenate([x, tail], axis=1)
        return x

    def load(t):
        rows = pl.ds(t * STEP, STEP)
        return pltpu.make_async_copy(pair.at[rows], pv.at[rows, pl.ds(0, C)], psem.at[t])

    @pl.loop(0, chunks)
    def _(t):
        load(t).start()

    qd_own = jnp.concatenate([q[...], d[...]], axis=1)
    kv_own = jnp.concatenate([k_in[...], v[...]], axis=1)
    qd[...] = qd_own
    kv[...] = kv_own
    qd_all[col] = qd_own
    kv_all[row] = kv_own
    greet(nrow, ncol, row, col)

    def line(src):
        return src * inner + b_in

    def pass_up(src, ref):
        return remote(ref, qd_all.at[line(src)], up_s.at[src], zr.at[src], row, col + inner)

    def pass_down(src, ref):
        return remote(ref, qd_all.at[line(src)], down_s.at[src], zr.at[src], row, col - inner)

    def pass_flip(src, ref):
        return remote(ref, qd_all.at[line(src)], fs.at[src], fr.at[src], row, flip)

    @pl.when(a + 1 < outer)
    def _():
        pass_up(a, qd).start()

    @pl.when(a > 0)
    def _():
        pass_down(a, qd).start()

    if inner == 2:
        pass_flip(a, qd).start()

    def kv_far(k):
        to = lax.rem(x_at + k, rout) * rin + core
        return remote(kv, kv_all.at[row], ks.at[k], kr.at[k], to, col)

    def kv_twin(k, ref):
        src = lax.rem(x_at + rout - k, rout) * rin + core
        return remote(ref, kv_all.at[src], js.at[k], jr.at[k], twin, col)

    for k in range(1, rout):
        kv_far(k).start()
    if rin == 2:
        kv_twin(0, kv).start()

    def arrive(j):
        @pl.when(a >= j)
        def _():
            src = a - j
            here = qd_all.at[line(src)]
            pass_up(src, here).wait_recv()

            @pl.when(a + 1 < outer)
            def _():
                pass_up(src, here).start()

            if inner == 2:
                pass_flip(src, here).start()

        @pl.when(a + j < outer)
        def _():
            src = a + j
            here = qd_all.at[line(src)]
            pass_down(src, here).wait_recv()

            @pl.when(a > 0)
            def _():
                pass_down(src, here).start()

            if inner == 2:
                pass_flip(src, here).start()

    def kv_arrive(k):
        src = lax.rem(x_at + rout - k, rout) * rin + core
        remote(kv, kv_all.at[src], ks.at[k], kr.at[k], row, col).wait_recv()
        if rin == 2:
            kv_twin(k, kv_all.at[src]).start()

    if Cp > C:
        pv[:, C:, :] = jnp.zeros((R, Cp - C, W), BF16)

    @pl.loop(0, chunks)
    def _(t):
        load(t).wait()
        for u in range(0, STEP, 2):
            i = t * STEP + u
            r = dot_nt(wt[...], pv[pl.ds(i, 2)].reshape(2 * Cp, W))
            bias[pl.ds(i, H, stride=R), :] = r[:, :Cp]
            bias[pl.ds(i + 1, H, stride=R), :] = r[:, Cp:]
        for j in range(1, outer):
            if HOP * j < chunks:

                @pl.when(t == HOP * j)
                def _():
                    arrive(j)

        if HOP < chunks:

            @pl.when(t == HOP)
            def _():
                for k in range(1, rout):
                    kv_arrive(k)

    if HOP >= chunks:
        for k in range(1, rout):
            kv_arrive(k)
    for j in range(1, outer):
        if HOP * j >= chunks:
            arrive(j)
    if rin == 2:
        for k in range(rout):
            src = lax.rem(x_at + rout - k, rout) * rin + rin - 1 - core
            remote(kv, kv_all.at[src], js.at[k], jr.at[k], row, col).wait_recv()

    @pl.loop(0, nrow)
    def _(r):
        x = kv_all[r].T
        kt[pl.ds(r * hr, hr)] = x[:drow].reshape(hr, HD, C)
        vt[pl.ds(r * hr, hr)] = x[drow:].reshape(hr, HD, C)

    lag = ncol // 2

    def combine():
        for k in range(1, ncol):
            src = lax.rem(col + k, ncol)
            remote(st.at[src], got.at[src], s1.at[src], r1.at[src], row, col).wait_recv()
        got[col] = st[col]
        sections = [(0, 0, hb)]
        if folded:
            sections.append((3 * hb, 2 * hb, hb // 2))
        for lo, out, n in sections:
            top = got[0, lo:lo + n]
            for k in range(1, ncol):
                top = jnp.maximum(top, got[k, lo:lo + n])
            total = jnp.zeros_like(top)
            upper = jnp.zeros_like(top)
            for k in range(ncol):
                scale = jnp.exp(got[k, lo:lo + n] - top)
                total += got[k, lo + n:lo + 2 * n] * scale
                upper += got[k, lo + 2 * n:lo + 3 * n] * scale
            delta = upper / total
            for k in range(ncol):
                back[k, out:out + n] = jnp.exp(got[k, lo:lo + n] - top) / total
                back[k, out + n:out + 2 * n] = delta
        bk[col] = back[col]
        for k in range(1, ncol):
            to = lax.rem(col + k, ncol)
            remote(back.at[to], bk.at[col], s2.at[to], r2.at[col], row, to).start()

    @pl.loop(0, ncol)
    def _(b):
        if inner == 2:

            @pl.when(lax.rem(b, inner) != b_in)
            def _():
                at = b // inner
                remote(qd, qd_all.at[b], fs.at[at], fr.at[at], row, col).wait_recv()

        x = qd_all[b].T
        qt[pl.ds(b * hb, hb)] = (x[:dcol] * jnp.asarray(SCALE, BF16)).reshape(hb, HD, R)
        dt[pl.ds(b * hb, hb)] = x[dcol:].reshape(hb, HD, R)
        heads = pl.ds(b * hb, hb)
        kb = kt[heads].reshape(dcol, C).T
        vb = vt[heads].reshape(dcol, C).T
        qb = qt[heads].reshape(dcol, R)
        db = dt[heads].reshape(dcol, R)
        owner = lax.broadcasted_iota(jnp.int32, (C, dcol), 1) // HD
        zero = jnp.zeros((C, dcol), BF16)
        for t in range(hb):
            h = b * hb + t
            term = bias[pl.ds(pl.multiple_of(h * R, 8), R), :].T[:C]
            s = dot(jnp.where(owner == t, kb, zero), qb) + term
            g = dot(jnp.where(owner == t, vb, zero), db)
            top = jnp.max(s, axis=0, keepdims=True)
            e = jnp.exp(s - top)
            e_buf[h] = e
            g_buf[h] = g
            put_row(st, b, t, 3 * hb, top)
            put_row(st, b, hb + t, 3 * hb, jnp.sum(e, axis=0, keepdims=True))
            put_row(st, b, 2 * hb + t, 3 * hb, jnp.sum(e * g, axis=0, keepdims=True))

        @pl.when(col != b)
        def _():
            remote(st.at[b], got.at[col], s1.at[b], r1.at[col], row, b).start()

        @pl.when(col == b - lag)
        def _():
            combine()

    per = hr // hb if hr % hb == 0 else 0

    def send_dkv(r):
        at = r // rin
        return remote(dkv.at[r], dkv_near.at[at], gn_s.at[at], gn_r.at[at], twin, col)

    def send_dq(b):
        at = b // inner
        return remote(dq.at[b], dq_near.at[at], qn_s.at[at], qn_r.at[at], row, flip)

    @pl.loop(0, ncol)
    def _(b):
        @pl.when(col == ncol - lag + b)
        def _():
            combine()

        @pl.when(col != b)
        def _():
            remote(back.at[b], bk.at[b], s2.at[b], r2.at[b], row, col).wait_recv()

        for t in range(hb):
            h = b * hb + t
            r = h // hr
            w = e_buf[h] * get_row(bk, b, t, 2 * hb)
            ds = (w * (g_buf[h] - get_row(bk, b, hb + t, 2 * hb))).astype(BF16)
            low = w.astype(BF16)
            y = (dot(kt[h], ds) * SCALE).astype(BF16)
            dq[b, t * HD:(t + 1) * HD, :] = y[:, :main_lanes]
            if folded:
                lo, at = dcol + (t // 2) * HD, (t % 2) * half
                dq[b, lo:lo + HD, at:at + half] = y[:, main_lanes:]
            dkv[r, 0, lax.rem(h, hr)] = dot_nt(qt[h], ds).astype(BF16)
            dkv[r, 1, lax.rem(h, hr)] = dot_nt(dt[h], low).astype(BF16)
            bias[pl.ds(pl.multiple_of(h * R, 8), R), pl.ds(0, C)] = ds.astype(F32).T

        if inner == 2:

            @pl.when(lax.rem(b, inner) != b_in)
            def _():
                send_dq(b).start()

        if per and rin == 2:
            done = b // per

            @pl.when(jnp.logical_and(lax.rem(b, per) == per - 1, lax.rem(done, rin) != core))
            def _():
                send_dkv(done).start()

    if not per and rin == 2:
        for x in range(rout):
            send_dkv(x * rin + rin - 1 - core).start()

    def merge_dq(at):
        value = dq[at * inner + b_in].astype(F32)
        if inner == 2:
            remote(dq.at[0], dq_near.at[at], qn_s.at[0], qn_r.at[at], row, col).wait_recv()
            value += dq_near[at].astype(F32)
        return value

    def merge_dkv(at):
        value = dkv[at * rin + core].astype(F32)
        if rin == 2:
            remote(dkv.at[0], dkv_near.at[at], gn_s.at[0], gn_r.at[at], row, col).wait_recv()
            value += dkv_near[at].astype(F32)
        return value

    def far_dq(at):
        to = at * inner + b_in
        return remote(dq.at[to], dq_far.at[a], qf_s.at[at], qf_r.at[a], row, to)

    def far_dkv(at):
        to = at * rin + core
        return remote(dkv.at[to], dkv_far.at[x_at], gf_s.at[at], gf_r.at[x_at], to, col)

    def merge():
        for k in range(1, outer):
            at = lax.rem(a + k, outer)
            dq[at * inner + b_in] = merge_dq(at).astype(BF16)
            far_dq(at).start()
        for k in range(1, rout):
            at = lax.rem(x_at + k, rout)
            dkv[at * rin + core] = merge_dkv(at).astype(BF16)
            far_dkv(at).start()

    acc[...] = jnp.zeros_like(acc)

    def rows_of(i):
        return bias[pl.ds(i, H, stride=R), :]

    def weight(t):
        total = acc[...]
        for u in range(0, STEP, 2):
            i = t * STEP + u
            lhs = jnp.concatenate(
                [rows_of(i).astype(BF16), rows_of(i + 1).astype(BF16)], axis=1
            )
            total = total + dot(lhs, pv[pl.ds(i, 2)].reshape(2 * Cp, W))
        acc[...] = total

    pl.loop(0, chunks // 2)(weight)
    merge()
    pl.loop(chunks // 2, chunks)(weight)

    for r in range(nrow):
        for b in range(ncol):
            wb[r, b] = acc[b * hb:(b + 1) * hb, r * wr:(r + 1) * wr].astype(BF16)

    def put(t, slot):
        return pltpu.make_async_copy(
            f_st.at[slot], f_out.at[pl.ds(t * STEP, STEP)], fsem.at[slot]
        )

    def flat(lo, hi):
        @pl.loop(lo, hi)
        def _(t):
            slot = lax.rem(t, SLOTS)

            @pl.when(t >= SLOTS)
            def _():
                put(t - SLOTS, slot).wait()

            for u in range(STEP):
                f_st[slot, u] = rows_of(t * STEP + u).T[:C].astype(BF16)
            put(t, slot).start()

    cuts = [0, chunks // 4, (2 * chunks) // 3, chunks - chunks // 8, chunks]

    for k in range(1, nrow):
        to = lax.rem(row + k, nrow)
        remote(wb.at[to], w1.at[k], ws1.at[k], wr1.at[k], to, col).start()
    flat(cuts[0], cuts[1])
    total = wb[row].astype(F32)
    for k in range(1, nrow):
        remote(wb.at[0], w1.at[k], ws1.at[k], wr1.at[k], row, col).wait_recv()
        total += w1[k].astype(F32)
    w1sum[...] = total
    for k in range(1, ncol):
        to = lax.rem(col + k, ncol)
        remote(w1sum.at[to], w2.at[k], ws2.at[k], wr2.at[k], row, to).start()
    flat(cuts[1], cuts[2])
    part = w1sum[col]
    for k in range(1, ncol):
        remote(w1sum.at[0], w2.at[k], ws2.at[k], wr2.at[k], row, col).wait_recv()
        part += w2[k]
    w2sum[...] = part
    wb_out[row, col] = part
    for k in range(1, ncol):
        to = lax.rem(col + k, ncol)
        remote(w2sum, wb_out.at[row, col], ws3.at[k], wr3.at[k], row, to).start()
    flat(cuts[2], cuts[3])

    grad = merge_dkv(x_at)
    for k in range(1, rout):
        src = lax.rem(x_at + k, rout)
        remote(dkv.at[0], dkv_far.at[src], gf_s.at[0], gf_r.at[src], row, col).wait_recv()
        grad += dkv_far[src].astype(F32)
    k_out[...] = grad[0].reshape(drow, C).T.astype(BF16)
    v_out[...] = grad[1].reshape(drow, C).T.astype(BF16)
    grad = merge_dq(a)
    for k in range(1, outer):
        src = lax.rem(a + k, outer)
        remote(dq.at[0], dq_far.at[src], qf_s.at[0], qf_r.at[src], row, col).wait_recv()
        grad += dq_far[src].astype(F32)
    if folded:
        tail = grad[dcol:].reshape(hb // 2, HD, LANES)
        tail = jnp.stack([tail[:, :, :half], tail[:, :, half:]], axis=1).reshape(dcol, half)
        q_out[:LANES] = grad[:dcol].T.astype(BF16)
        q_out[LANES:] = tail.T.astype(BF16)
    else:
        q_out[...] = grad.T.astype(BF16)

    for k in range(1, ncol):
        src = lax.rem(col + ncol - k, ncol)
        remote(w2sum, wb_out.at[row, src], ws3.at[k], wr3.at[k], row, col).wait_recv()
    for k in range(1, nrow):
        to = lax.rem(row + k, nrow)
        remote(wb_out.at[row], wb_out.at[row], ws4.at[k], wr4.at[k], to, col).start()
    flat(cuts[3], cuts[4])
    for k in range(1, nrow):
        src = lax.rem(row + nrow - k, nrow)
        remote(wb_out.at[src], wb_out.at[src], ws4.at[k], wr4.at[k], row, col).wait_recv()

    for t in range(max(0, chunks - SLOTS), chunks):
        put(t, t % SLOTS).wait()
    for src in range(outer):

        @pl.when(jnp.logical_and(a >= src, a + 1 < outer))
        def _():
            pass_up(src, qd).wait_send()

        @pl.when(jnp.logical_and(a <= src, a > 0))
        def _():
            pass_down(src, qd).wait_send()

        if inner == 2:
            pass_flip(src, qd).wait_send()
            send_dq(src * inner + 1 - b_in).wait_send()
    for k in range(rout):
        if rin == 2:
            kv_twin(k, kv).wait_send()
            send_dkv(k * rin + 1 - core).wait_send()
        if k:
            kv_far(k).wait_send()
            far_dkv(lax.rem(x_at + k, rout)).wait_send()
    for k in range(1, outer):
        far_dq(lax.rem(a + k, outer)).wait_send()
    for k in range(1, ncol):
        to = lax.rem(col + k, ncol)
        remote(st.at[to], got.at[col], s1.at[to], r1.at[col], row, to).wait_send()
        remote(back.at[to], bk.at[col], s2.at[to], r2.at[col], row, to).wait_send()
        remote(w1sum.at[to], w2.at[k], ws2.at[k], wr2.at[k], row, to).wait_send()
        remote(w2sum, wb_out.at[row, col], ws3.at[k], wr3.at[k], row, to).wait_send()
    for k in range(1, nrow):
        to = lax.rem(row + k, nrow)
        remote(wb.at[to], w1.at[k], ws1.at[k], wr1.at[k], to, col).wait_send()
        remote(wb_out.at[row], wb_out.at[row], ws4.at[k], wr4.at[k], to, col).wait_send()


def main(nrow, ncol, wt, pair, q, k, v, d):
    R, C, W = pair.shape
    H = wt.shape[0]
    hb, hr = H // ncol, H // nrow
    dcol, drow = q.shape[1], k.shape[1]
    Cp = -(-C // LANES) * LANES
    wr = W // nrow
    shape = jax.ShapeDtypeStruct
    (inner, outer), (rin, rout) = split(ncol), split(nrow)
    folded, _ = folds(R, hb)
    width = LANES if folded else R
    extra = 3 * hb // 2 if folded else 0
    dq_rows = dcol + (dcol // 2 if folded else 0)
    return pl.pallas_call(
        functools.partial(main_kernel, nrow, ncol),
        out_shape=(
            shape((R, C, H), BF16),
            shape((nrow, ncol, hb, wr), F32),
            shape((R, dcol), BF16),
            shape((C, drow), BF16),
            shape((C, drow), BF16),
        ),
        in_specs=[pl.BlockSpec(memory_space=VMEM), pl.BlockSpec(memory_space=pl.ANY)]
        + [pl.BlockSpec(memory_space=VMEM)] * 4,
        out_specs=[pl.BlockSpec(memory_space=pl.ANY)] + [pl.BlockSpec(memory_space=VMEM)] * 4,
        scratch_shapes=[
            VMEM((R, Cp, W), BF16),
            VMEM((H * R, Cp), F32),
            VMEM((H, C, R), F32),
            VMEM((H, C, R), F32),
            VMEM((R, 2 * dcol), BF16),
            VMEM((C, 2 * drow), BF16),
            VMEM((ncol, R, 2 * dcol), BF16),
            VMEM((nrow, C, 2 * drow), BF16),
            VMEM((H, HD, R), BF16),
            VMEM((H, HD, R), BF16),
            VMEM((H, HD, C), BF16),
            VMEM((H, HD, C), BF16),
            VMEM((ncol, 3 * hb + extra, width), F32),
            VMEM((ncol, 3 * hb + extra, width), F32),
            VMEM((ncol, 2 * hb + (hb if folded else 0), width), F32),
            VMEM((ncol, 2 * hb + (hb if folded else 0), width), F32),
            VMEM((ncol, dq_rows, width), BF16),
            VMEM((outer, dq_rows, width), BF16),
            VMEM((outer, dq_rows, width), BF16),
            VMEM((nrow, 2, hr, HD, C), BF16),
            VMEM((rout, 2, hr, HD, C), BF16),
            VMEM((rout, 2, hr, HD, C), BF16),
            VMEM((H, W), F32),
            VMEM((nrow, ncol, hb, wr), BF16),
            VMEM((nrow, ncol, hb, wr), BF16),
            VMEM((ncol, hb, wr), F32),
            VMEM((ncol, hb, wr), F32),
            VMEM((hb, wr), F32),
            VMEM((SLOTS, STEP, C, H), BF16),
            DMA((R // STEP,)),
            DMA((outer,)), DMA((outer,)), DMA((outer,)), DMA((outer,)), DMA((outer,)),
            DMA((rout,)), DMA((rout,)), DMA((rout,)), DMA((rout,)),
            DMA((ncol,)), DMA((ncol,)), DMA((ncol,)), DMA((ncol,)),
            DMA((outer,)), DMA((outer,)), DMA((outer,)), DMA((outer,)),
            DMA((rout,)), DMA((rout,)), DMA((rout,)), DMA((rout,)),
            DMA((nrow,)), DMA((nrow,)), DMA((ncol,)), DMA((ncol,)),
            DMA((ncol,)), DMA((ncol,)), DMA((nrow,)), DMA((nrow,)),
            DMA((SLOTS,)),
        ],
        compiler_params=pltpu.CompilerParams(
            collective_id=0, has_side_effects=True, vmem_limit_bytes=67043328
        ),
    )(wt, pair, q, k, v, d)


def finish_kernel(f, wt, wb, q, k, v, d_pair, wo, qo, ko, vo):
    rows, C, H = f.shape
    d_pair[...] = dot(f[...].reshape(rows * C, H), wt[...]).astype(BF16).reshape(d_pair.shape)

    @pl.when(pl.program_id(0) == 0)
    def _():
        qo[...] = q[...]
        ko[...] = k[...]
        vo[...] = v[...]
        nrow, wr = wb.shape[0], wb.shape[3]
        for r in range(nrow):
            wo[:, r * wr:(r + 1) * wr] = wb[r].reshape(H, wr)


def finish(f, wt, wb, q, k, v):
    R, C, H = f.shape
    block = 3 * STEP if R % (3 * STEP) == 0 else STEP
    W = wt.shape[1]

    def whole(x):
        return pl.BlockSpec(x.shape, lambda i: (0,) * len(x.shape))

    return pl.pallas_call(
        finish_kernel,
        grid=(R // block,),
        out_shape=(
            jax.ShapeDtypeStruct((R, C, W), BF16),
            jax.ShapeDtypeStruct((H, W), F32),
            jax.ShapeDtypeStruct(q.shape, BF16),
            jax.ShapeDtypeStruct(k.shape, BF16),
            jax.ShapeDtypeStruct(v.shape, BF16),
        ),
        in_specs=[pl.BlockSpec((block, C, H), lambda i: (i, 0, 0))]
        + [whole(x) for x in (wt, wb, q, k, v)],
        out_specs=(
            pl.BlockSpec((block, C, W), lambda i: (i, 0, 0)),
            pl.BlockSpec((H, W), lambda i: (0, 0)),
            whole(q), whole(k), whole(v),
        ),
    )(f, wt, wb, q, k, v)


def on_device(nrow, ncol, pair, w_bias, queries, keys, values, d_out):
    wt = w_bias.T
    f, wb, q, k, v = main(nrow, ncol, wt, pair, queries, keys, values, d_out)
    d_pair, d_wbias, d_queries, d_keys, d_values = finish(f, wt, wb, q, k, v)
    return d_pair, d_wbias.T, d_queries, d_keys, d_values


def solution(mesh):
    return jax.shard_map(
        functools.partial(on_device, mesh.shape["row"], mesh.shape["col"]),
        mesh=mesh,
        in_specs=(
            P("row", "col", None),
            P(),
            P("row", "col"),
            P("col", "row"),
            P("col", "row"),
            P("row", "col"),
        ),
        out_specs=(P("row", "col", None), P(), P("row", "col"), P("col", "row"), P("col", "row")),
        check_vma=False,
    )
```

```python
import functools

import jax
import jax.numpy as jnp
from jax import lax
from jax.experimental import pallas as pl
from jax.experimental.pallas import tpu as pltpu
from jax.sharding import PartitionSpec as P

HD = 16
SCALE = 1.0 / HD**0.5
LANES = 128
STEP = 16
SLOTS = 2
HOP = 4
MESH = pl.DeviceIdType.MESH
VMEM = pltpu.VMEM
DMA = pltpu.SemaphoreType.DMA
F32 = jnp.float32
BF16 = jnp.bfloat16


def remote(src, dst, send, recv, row, col):
    return pltpu.make_async_remote_copy(
        src_ref=src, dst_ref=dst, send_sem=send, recv_sem=recv,
        device_id=(row, col), device_id_type=MESH,
    )


def split(n):
    return (2, n // 2) if n % 2 == 0 else (1, n)


def folds(R, hb):
    half = R % LANES
    return R == LANES + half and 2 * half == LANES and hb % 2 == 0, half


def greet(nrow, ncol, row, col):
    barrier = pltpu.get_barrier_semaphore()
    for k in range(1, ncol):
        pl.semaphore_signal(
            barrier, inc=1, device_id=(row, lax.rem(col + k, ncol)), device_id_type=MESH
        )
    for k in range(1, nrow):
        pl.semaphore_signal(
            barrier, inc=1, device_id=(lax.rem(row + k, nrow), col), device_id_type=MESH
        )
    pl.semaphore_wait(barrier, ncol + nrow - 2)


def dot(a, b):
    return jnp.dot(a, b, preferred_element_type=F32)


def dot_nt(a, b):
    return lax.dot_general(a, b, (((1,), (1,)), ((), ())), preferred_element_type=F32)


def main_kernel(
    nrow, ncol, wt, pair, q, k_in, v, d,
    f_out, wb_out, q_out, k_out, v_out,
    pv, bias, e_buf, g_buf, qd, kv, qd_all, kv_all, qt, dt, kt, vt,
    st, got, back, bk, dq, dq_near, dq_far, dkv, dkv_near, dkv_far,
    acc, wb, w1, w1sum, w2, w2sum, f_st,
    psem, up_s, down_s, zr, fs, fr, ks, kr, js, jr, s1, r1, s2, r2,
    qn_s, qn_r, qf_s, qf_r, gn_s, gn_r, gf_s, gf_r,
    ws1, wr1, ws2, wr2, ws3, wr3, ws4, wr4, fsem,
):
    row, col = lax.axis_index("row"), lax.axis_index("col")
    R, C, W = pair.shape
    H = wt.shape[0]
    Cp = pv.shape[1]
    hb, hr = H // ncol, H // nrow
    dcol, drow = hb * HD, hr * HD
    wr = W // nrow
    chunks = R // STEP
    inner, outer, rin, rout = split(ncol) + split(nrow)
    a, b_in = col // inner, lax.rem(col, inner)
    flip = a * inner + inner - 1 - b_in
    x_at, core = row // rin, lax.rem(row, rin)
    twin = x_at * rin + rin - 1 - core
    upper_half = (2 * a) // outer
    slot = b_in * outer + (1 - upper_half) * 2 * a + upper_half * (2 * (outer - a) - 1)

    def block_at(p):
        q = lax.rem(p, outer)
        odd = lax.rem(q, 2)
        end = (1 - odd) * (q // 2) + odd * (outer - 1 - q // 2)
        return end * inner + p // outer

    folded, half = folds(R, hb)
    main_lanes = LANES if folded else R

    def put_row(ref, b, s, n, x):
        ref[b, s:s + 1, :] = x[:, :main_lanes]
        if folded:
            at = (s % 2) * half
            ref[b, n + s // 2:n + s // 2 + 1, at:at + half] = x[:, main_lanes:]

    def get_row(ref, b, s, n):
        x = ref[b, s:s + 1, :]
        if folded:
            at = (s % 2) * half
            tail = ref[b, n + s // 2:n + s // 2 + 1, at:at + half]
            x = jnp.concatenate([x, tail], axis=1)
        return x

    def load(t):
        rows = pl.ds(t * STEP, STEP)
        return pltpu.make_async_copy(pair.at[rows], pv.at[rows, pl.ds(0, C)], psem.at[t])

    @pl.loop(0, chunks)
    def _(t):
        load(t).start()

    qd_own = jnp.concatenate([q[...], d[...]], axis=1)
    kv_own = jnp.concatenate([k_in[...], v[...]], axis=1)
    qd[...] = qd_own
    kv[...] = kv_own
    qd_all[col] = qd_own
    kv_all[row] = kv_own
    greet(nrow, ncol, row, col)

    def line(src):
        return src * inner + b_in

    def pass_up(src, ref):
        return remote(ref, qd_all.at[line(src)], up_s.at[src], zr.at[src], row, col + inner)

    def pass_down(src, ref):
        return remote(ref, qd_all.at[line(src)], down_s.at[src], zr.at[src], row, col - inner)

    def pass_flip(src, ref):
        return remote(ref, qd_all.at[line(src)], fs.at[src], fr.at[src], row, flip)

    @pl.when(a + 1 < outer)
    def _():
        pass_up(a, qd).start()

    @pl.when(a > 0)
    def _():
        pass_down(a, qd).start()

    if inner == 2:
        pass_flip(a, qd).start()

    def kv_far(k):
        to = lax.rem(x_at + k, rout) * rin + core
        return remote(kv, kv_all.at[row], ks.at[k], kr.at[k], to, col)

    def kv_twin(k, ref):
        src = lax.rem(x_at + rout - k, rout) * rin + core
        return remote(ref, kv_all.at[src], js.at[k], jr.at[k], twin, col)

    for k in range(1, rout):
        kv_far(k).start()
    if rin == 2:
        kv_twin(0, kv).start()

    def arrive(j):
        @pl.when(a >= j)
        def _():
            src = a - j
            here = qd_all.at[line(src)]
            pass_up(src, here).wait_recv()

            @pl.when(a + 1 < outer)
            def _():
                pass_up(src, here).start()

            if inner == 2:
                pass_flip(src, here).start()

        @pl.when(a + j < outer)
        def _():
            src = a + j
            here = qd_all.at[line(src)]
            pass_down(src, here).wait_recv()

            @pl.when(a > 0)
            def _():
                pass_down(src, here).start()

            if inner == 2:
                pass_flip(src, here).start()

    def kv_arrive(k):
        src = lax.rem(x_at + rout - k, rout) * rin + core
        remote(kv, kv_all.at[src], ks.at[k], kr.at[k], row, col).wait_recv()
        if rin == 2:
            kv_twin(k, kv_all.at[src]).start()

    if Cp > C:
        pv[:, C:, :] = jnp.zeros((R, Cp - C, W), BF16)

    @pl.loop(0, chunks)
    def _(t):
        load(t).wait()
        for u in range(0, STEP, 2):
            i = t * STEP + u
            r = dot_nt(wt[...], pv[pl.ds(i, 2)].reshape(2 * Cp, W))
            bias[pl.ds(i, H, stride=R), :] = r[:, :Cp]
            bias[pl.ds(i + 1, H, stride=R), :] = r[:, Cp:]
        for j in range(1, outer):
            if HOP * j < chunks:

                @pl.when(t == HOP * j)
                def _():
                    arrive(j)

        if HOP < chunks:

            @pl.when(t == HOP)
            def _():
                for k in range(1, rout):
                    kv_arrive(k)

    if HOP >= chunks:
        for k in range(1, rout):
            kv_arrive(k)
    for j in range(1, outer):
        if HOP * j >= chunks:
            arrive(j)
    if rin == 2:
        for k in range(rout):
            src = lax.rem(x_at + rout - k, rout) * rin + rin - 1 - core
            remote(kv, kv_all.at[src], js.at[k], jr.at[k], row, col).wait_recv()

    @pl.loop(0, nrow)
    def _(r):
        x = kv_all[r].T
        kt[pl.ds(r * hr, hr)] = x[:drow].reshape(hr, HD, C)
        vt[pl.ds(r * hr, hr)] = x[drow:].reshape(hr, HD, C)

    lag = ncol // 2

    def combine():
        for k in range(1, ncol):
            src = lax.rem(col + k, ncol)
            remote(st.at[src], got.at[src], s1.at[src], r1.at[src], row, col).wait_recv()
        got[col] = st[col]
        sections = [(0, 0, hb)]
        if folded:
            sections.append((3 * hb, 2 * hb, hb // 2))
        for lo, out, n in sections:
            top = got[0, lo:lo + n]
            for k in range(1, ncol):
                top = jnp.maximum(top, got[k, lo:lo + n])
            total = jnp.zeros_like(top)
            upper = jnp.zeros_like(top)
            for k in range(ncol):
                scale = jnp.exp(got[k, lo:lo + n] - top)
                total += got[k, lo + n:lo + 2 * n] * scale
                upper += got[k, lo + 2 * n:lo + 3 * n] * scale
            delta = upper / total
            for k in range(ncol):
                back[k, out:out + n] = jnp.exp(got[k, lo:lo + n] - top) / total
                back[k, out + n:out + 2 * n] = delta
        bk[col] = back[col]
        for k in range(1, ncol):
            to = lax.rem(col + k, ncol)
            remote(back.at[to], bk.at[col], s2.at[to], r2.at[col], row, to).start()

    @pl.loop(0, ncol)
    def _(p):
        b = block_at(p)
        if inner == 2:

            @pl.when(lax.rem(b, inner) != b_in)
            def _():
                at = b // inner
                remote(qd, qd_all.at[b], fs.at[at], fr.at[at], row, col).wait_recv()

        x = qd_all[b].T
        qt[pl.ds(b * hb, hb)] = (x[:dcol] * jnp.asarray(SCALE, BF16)).reshape(hb, HD, R)
        dt[pl.ds(b * hb, hb)] = x[dcol:].reshape(hb, HD, R)
        heads = pl.ds(b * hb, hb)
        kb = kt[heads].reshape(dcol, C).T
        vb = vt[heads].reshape(dcol, C).T
        qb = qt[heads].reshape(dcol, R)
        db = dt[heads].reshape(dcol, R)
        owner = lax.broadcasted_iota(jnp.int32, (C, dcol), 1) // HD
        zero = jnp.zeros((C, dcol), BF16)
        for t in range(hb):
            h = b * hb + t
            term = bias[pl.ds(pl.multiple_of(h * R, 8), R), :].T[:C]
            s = dot(jnp.where(owner == t, kb, zero), qb) + term
            g = dot(jnp.where(owner == t, vb, zero), db)
            top = jnp.max(s, axis=0, keepdims=True)
            e = jnp.exp(s - top)
            e_buf[h] = e
            g_buf[h] = g
            put_row(st, b, t, 3 * hb, top)
            put_row(st, b, hb + t, 3 * hb, jnp.sum(e, axis=0, keepdims=True))
            put_row(st, b, 2 * hb + t, 3 * hb, jnp.sum(e * g, axis=0, keepdims=True))

        @pl.when(col != b)
        def _():
            remote(st.at[b], got.at[col], s1.at[b], r1.at[col], row, b).start()

        @pl.when(slot == p - lag)
        def _():
            combine()

    def send_dkv(r):
        at = r // rin
        return remote(dkv.at[r], dkv_near.at[at], gn_s.at[at], gn_r.at[at], twin, col)

    def send_dq(b):
        at = b // inner
        return remote(dq.at[b], dq_near.at[at], qn_s.at[at], qn_r.at[at], row, flip)

    @pl.loop(0, ncol)
    def _(p):
        b = block_at(p)

        @pl.when(slot == ncol - lag + p)
        def _():
            combine()

        @pl.when(col != b)
        def _():
            remote(back.at[b], bk.at[b], s2.at[b], r2.at[b], row, col).wait_recv()

        for t in range(hb):
            h = b * hb + t
            r = h // hr
            w = e_buf[h] * get_row(bk, b, t, 2 * hb)
            ds = (w * (g_buf[h] - get_row(bk, b, hb + t, 2 * hb))).astype(BF16)
            low = w.astype(BF16)
            y = (dot(kt[h], ds) * SCALE).astype(BF16)
            dq[b, t * HD:(t + 1) * HD, :] = y[:, :main_lanes]
            if folded:
                lo, at = dcol + (t // 2) * HD, (t % 2) * half
                dq[b, lo:lo + HD, at:at + half] = y[:, main_lanes:]
            dkv[r, 0, lax.rem(h, hr)] = dot_nt(qt[h], ds).astype(BF16)
            dkv[r, 1, lax.rem(h, hr)] = dot_nt(dt[h], low).astype(BF16)
            bias[pl.ds(pl.multiple_of(h * R, 8), R), pl.ds(0, C)] = ds.astype(F32).T

        if inner == 2:

            @pl.when(lax.rem(b, inner) != b_in)
            def _():
                send_dq(b).start()

    if rin == 2:
        for x in range(rout):
            send_dkv(x * rin + rin - 1 - core).start()

    def merge_dq(at):
        value = dq[at * inner + b_in].astype(F32)
        if inner == 2:
            remote(dq.at[0], dq_near.at[at], qn_s.at[0], qn_r.at[at], row, col).wait_recv()
            value += dq_near[at].astype(F32)
        return value

    def merge_dkv(at):
        value = dkv[at * rin + core].astype(F32)
        if rin == 2:
            remote(dkv.at[0], dkv_near.at[at], gn_s.at[0], gn_r.at[at], row, col).wait_recv()
            value += dkv_near[at].astype(F32)
        return value

    def far_dq(at):
        to = at * inner + b_in
        return remote(dq.at[to], dq_far.at[a], qf_s.at[at], qf_r.at[a], row, to)

    def far_dkv(at):
        to = at * rin + core
        return remote(dkv.at[to], dkv_far.at[x_at], gf_s.at[at], gf_r.at[x_at], to, col)

    def merge():
        for k in range(1, outer):
            at = lax.rem(a + k, outer)
            dq[at * inner + b_in] = merge_dq(at).astype(BF16)
            far_dq(at).start()
        for k in range(1, rout):
            at = lax.rem(x_at + k, rout)
            dkv[at * rin + core] = merge_dkv(at).astype(BF16)
            far_dkv(at).start()

    acc[...] = jnp.zeros_like(acc)

    def rows_of(i):
        return bias[pl.ds(i, H, stride=R), :]

    wide = 2 * STEP if R % (4 * STEP) == 0 else STEP
    laps = R // wide

    def weight(t):
        total = acc[...]
        for u in range(0, wide, 2):
            i = t * wide + u
            lhs = jnp.concatenate(
                [rows_of(i).astype(BF16), rows_of(i + 1).astype(BF16)], axis=1
            )
            total = total + dot(lhs, pv[pl.ds(i, 2)].reshape(2 * Cp, W))
        acc[...] = total

    pl.loop(0, laps // 2)(weight)
    merge()
    pl.loop(laps // 2, laps)(weight)

    for r in range(nrow):
        for b in range(ncol):
            wb[r, b] = acc[b * hb:(b + 1) * hb, r * wr:(r + 1) * wr].astype(BF16)

    def put(t, slot):
        return pltpu.make_async_copy(
            f_st.at[slot], f_out.at[pl.ds(t * STEP, STEP)], fsem.at[slot]
        )

    def flat(lo, hi):
        @pl.loop(lo, hi)
        def _(t):
            slot = lax.rem(t, SLOTS)

            @pl.when(t >= SLOTS)
            def _():
                put(t - SLOTS, slot).wait()

            for u in range(STEP):
                f_st[slot, u] = rows_of(t * STEP + u).T[:C].astype(BF16)
            put(t, slot).start()

    cuts = [0, chunks // 4, (2 * chunks) // 3, chunks - chunks // 8, chunks]

    for k in range(1, nrow):
        to = lax.rem(row + k, nrow)
        remote(wb.at[to], w1.at[k], ws1.at[k], wr1.at[k], to, col).start()
    flat(cuts[0], cuts[1])
    total = wb[row].astype(F32)
    for k in range(1, nrow):
        remote(wb.at[0], w1.at[k], ws1.at[k], wr1.at[k], row, col).wait_recv()
        total += w1[k].astype(F32)
    w1sum[...] = total
    for k in range(1, ncol):
        to = lax.rem(col + k, ncol)
        remote(w1sum.at[to], w2.at[k], ws2.at[k], wr2.at[k], row, to).start()
    flat(cuts[1], cuts[2])
    part = w1sum[col]
    for k in range(1, ncol):
        remote(w1sum.at[0], w2.at[k], ws2.at[k], wr2.at[k], row, col).wait_recv()
        part += w2[k]
    part = part.astype(BF16)
    w2sum[...] = part
    wb_out[row, col] = part
    for k in range(1, ncol):
        to = lax.rem(col + k, ncol)
        remote(w2sum, wb_out.at[row, col], ws3.at[k], wr3.at[k], row, to).start()
    flat(cuts[2], cuts[3])

    grad = merge_dkv(x_at)
    for k in range(1, rout):
        src = lax.rem(x_at + k, rout)
        remote(dkv.at[0], dkv_far.at[src], gf_s.at[0], gf_r.at[src], row, col).wait_recv()
        grad += dkv_far[src].astype(F32)
    k_out[...] = grad[0].reshape(drow, C).T.astype(BF16)
    v_out[...] = grad[1].reshape(drow, C).T.astype(BF16)
    grad = merge_dq(a)
    for k in range(1, outer):
        src = lax.rem(a + k, outer)
        remote(dq.at[0], dq_far.at[src], qf_s.at[0], qf_r.at[src], row, col).wait_recv()
        grad += dq_far[src].astype(F32)
    if folded:
        tail = grad[dcol:].reshape(hb // 2, HD, LANES)
        tail = jnp.stack([tail[:, :, :half], tail[:, :, half:]], axis=1).reshape(dcol, half)
        q_out[:LANES] = grad[:dcol].T.astype(BF16)
        q_out[LANES:] = tail.T.astype(BF16)
    else:
        q_out[...] = grad.T.astype(BF16)

    for k in range(1, ncol):
        src = lax.rem(col + ncol - k, ncol)
        remote(w2sum, wb_out.at[row, src], ws3.at[k], wr3.at[k], row, col).wait_recv()
    for k in range(1, nrow):
        to = lax.rem(row + k, nrow)
        remote(wb_out.at[row], wb_out.at[row], ws4.at[k], wr4.at[k], to, col).start()
    flat(cuts[3], cuts[4])
    for k in range(1, nrow):
        src = lax.rem(row + nrow - k, nrow)
        remote(wb_out.at[src], wb_out.at[src], ws4.at[k], wr4.at[k], row, col).wait_recv()

    for t in range(max(0, chunks - SLOTS), chunks):
        put(t, t % SLOTS).wait()
    for src in range(outer):

        @pl.when(jnp.logical_and(a >= src, a + 1 < outer))
        def _():
            pass_up(src, qd).wait_send()

        @pl.when(jnp.logical_and(a <= src, a > 0))
        def _():
            pass_down(src, qd).wait_send()

        if inner == 2:
            pass_flip(src, qd).wait_send()
            send_dq(src * inner + 1 - b_in).wait_send()
    for k in range(rout):
        if rin == 2:
            kv_twin(k, kv).wait_send()
            send_dkv(k * rin + 1 - core).wait_send()
        if k:
            kv_far(k).wait_send()
            far_dkv(lax.rem(x_at + k, rout)).wait_send()
    for k in range(1, outer):
        far_dq(lax.rem(a + k, outer)).wait_send()
    for k in range(1, ncol):
        to = lax.rem(col + k, ncol)
        remote(st.at[to], got.at[col], s1.at[to], r1.at[col], row, to).wait_send()
        remote(back.at[to], bk.at[col], s2.at[to], r2.at[col], row, to).wait_send()
        remote(w1sum.at[to], w2.at[k], ws2.at[k], wr2.at[k], row, to).wait_send()
        remote(w2sum, wb_out.at[row, col], ws3.at[k], wr3.at[k], row, to).wait_send()
    for k in range(1, nrow):
        to = lax.rem(row + k, nrow)
        remote(wb.at[to], w1.at[k], ws1.at[k], wr1.at[k], to, col).wait_send()
        remote(wb_out.at[row], wb_out.at[row], ws4.at[k], wr4.at[k], to, col).wait_send()


def main(nrow, ncol, wt, pair, q, k, v, d):
    R, C, W = pair.shape
    H = wt.shape[0]
    hb, hr = H // ncol, H // nrow
    dcol, drow = q.shape[1], k.shape[1]
    Cp = -(-C // LANES) * LANES
    wr = W // nrow
    shape = jax.ShapeDtypeStruct
    (inner, outer), (rin, rout) = split(ncol), split(nrow)
    folded, _ = folds(R, hb)
    width = LANES if folded else R
    extra = 3 * hb // 2 if folded else 0
    dq_rows = dcol + (dcol // 2 if folded else 0)
    return pl.pallas_call(
        functools.partial(main_kernel, nrow, ncol),
        out_shape=(
            shape((R, C, H), BF16),
            shape((nrow, ncol, hb, wr), BF16),
            shape((R, dcol), BF16),
            shape((C, drow), BF16),
            shape((C, drow), BF16),
        ),
        in_specs=[pl.BlockSpec(memory_space=VMEM), pl.BlockSpec(memory_space=pl.ANY)]
        + [pl.BlockSpec(memory_space=VMEM)] * 4,
        out_specs=[pl.BlockSpec(memory_space=pl.ANY)] + [pl.BlockSpec(memory_space=VMEM)] * 4,
        scratch_shapes=[
            VMEM((R, Cp, W), BF16),
            VMEM((H * R, Cp), F32),
            VMEM((H, C, R), F32),
            VMEM((H, C, R), F32),
            VMEM((R, 2 * dcol), BF16),
            VMEM((C, 2 * drow), BF16),
            VMEM((ncol, R, 2 * dcol), BF16),
            VMEM((nrow, C, 2 * drow), BF16),
            VMEM((H, HD, R), BF16),
            VMEM((H, HD, R), BF16),
            VMEM((H, HD, C), BF16),
            VMEM((H, HD, C), BF16),
            VMEM((ncol, 3 * hb + extra, width), F32),
            VMEM((ncol, 3 * hb + extra, width), F32),
            VMEM((ncol, 2 * hb + (hb if folded else 0), width), F32),
            VMEM((ncol, 2 * hb + (hb if folded else 0), width), F32),
            VMEM((ncol, dq_rows, width), BF16),
            VMEM((outer, dq_rows, width), BF16),
            VMEM((outer, dq_rows, width), BF16),
            VMEM((nrow, 2, hr, HD, C), BF16),
            VMEM((rout, 2, hr, HD, C), BF16),
            VMEM((rout, 2, hr, HD, C), BF16),
            VMEM((H, W), F32),
            VMEM((nrow, ncol, hb, wr), BF16),
            VMEM((nrow, ncol, hb, wr), BF16),
            VMEM((ncol, hb, wr), F32),
            VMEM((ncol, hb, wr), F32),
            VMEM((hb, wr), BF16),
            VMEM((SLOTS, STEP, C, H), BF16),
            DMA((R // STEP,)),
            DMA((outer,)), DMA((outer,)), DMA((outer,)), DMA((outer,)), DMA((outer,)),
            DMA((rout,)), DMA((rout,)), DMA((rout,)), DMA((rout,)),
            DMA((ncol,)), DMA((ncol,)), DMA((ncol,)), DMA((ncol,)),
            DMA((outer,)), DMA((outer,)), DMA((outer,)), DMA((outer,)),
            DMA((rout,)), DMA((rout,)), DMA((rout,)), DMA((rout,)),
            DMA((nrow,)), DMA((nrow,)), DMA((ncol,)), DMA((ncol,)),
            DMA((ncol,)), DMA((ncol,)), DMA((nrow,)), DMA((nrow,)),
            DMA((SLOTS,)),
        ],
        compiler_params=pltpu.CompilerParams(
            collective_id=0, has_side_effects=True, vmem_limit_bytes=67043328
        ),
    )(wt, pair, q, k, v, d)


def finish_kernel(f, wt, wb, q, k, v, d_pair, wo, qo, ko, vo):
    rows, C, H = f.shape
    d_pair[...] = dot(f[...].reshape(rows * C, H), wt[...]).astype(BF16).reshape(d_pair.shape)

    @pl.when(pl.program_id(0) == 0)
    def _():
        qo[...] = q[...]
        ko[...] = k[...]
        vo[...] = v[...]
        nrow, wr = wb.shape[0], wb.shape[3]
        for r in range(nrow):
            wo[:, r * wr:(r + 1) * wr] = wb[r].astype(F32).reshape(H, wr)


def finish(f, wt, wb, q, k, v):
    R, C, H = f.shape
    block = 3 * STEP if R % (3 * STEP) == 0 else STEP
    W = wt.shape[1]

    def whole(x):
        return pl.BlockSpec(x.shape, lambda i: (0,) * len(x.shape))

    return pl.pallas_call(
        finish_kernel,
        grid=(R // block,),
        out_shape=(
            jax.ShapeDtypeStruct((R, C, W), BF16),
            jax.ShapeDtypeStruct((H, W), F32),
            jax.ShapeDtypeStruct(q.shape, BF16),
            jax.ShapeDtypeStruct(k.shape, BF16),
            jax.ShapeDtypeStruct(v.shape, BF16),
        ),
        in_specs=[pl.BlockSpec((block, C, H), lambda i: (i, 0, 0))]
        + [whole(x) for x in (wt, wb, q, k, v)],
        out_specs=(
            pl.BlockSpec((block, C, W), lambda i: (i, 0, 0)),
            pl.BlockSpec((H, W), lambda i: (0, 0)),
            whole(q), whole(k), whole(v),
        ),
    )(f, wt, wb, q, k, v)


def on_device(nrow, ncol, pair, w_bias, queries, keys, values, d_out):
    wt = w_bias.T
    f, wb, q, k, v = main(nrow, ncol, wt, pair, queries, keys, values, d_out)
    d_pair, d_wbias, d_queries, d_keys, d_values = finish(f, wt, wb, q, k, v)
    return d_pair, d_wbias.T, d_queries, d_keys, d_values


def solution(mesh):
    return jax.shard_map(
        functools.partial(on_device, mesh.shape["row"], mesh.shape["col"]),
        mesh=mesh,
        in_specs=(
            P("row", "col", None),
            P(),
            P("row", "col"),
            P("col", "row"),
            P("col", "row"),
            P("row", "col"),
        ),
        out_specs=(P("row", "col", None), P(), P("row", "col"), P("col", "row"), P("col", "row")),
        check_vma=False,
    )
```

```python
import functools

import jax
import jax.numpy as jnp
from jax import lax
from jax.experimental import pallas as pl
from jax.experimental.pallas import tpu as pltpu
from jax.sharding import PartitionSpec as P

HD = 16
SCALE = 1.0 / HD**0.5
LANES = 128
STEP = 16
SLOTS = 2
HOP = 4
MESH = pl.DeviceIdType.MESH
VMEM = pltpu.VMEM
DMA = pltpu.SemaphoreType.DMA
F32 = jnp.float32
BF16 = jnp.bfloat16


def remote(src, dst, send, recv, row, col):
    return pltpu.make_async_remote_copy(
        src_ref=src, dst_ref=dst, send_sem=send, recv_sem=recv,
        device_id=(row, col), device_id_type=MESH,
    )


def split(n):
    return (2, n // 2) if n % 2 == 0 else (1, n)


def folds(R, hb):
    half = R % LANES
    return R == LANES + half and 2 * half == LANES and hb % 2 == 0, half


def greet(nrow, ncol, row, col):
    barrier = pltpu.get_barrier_semaphore()
    for k in range(1, ncol):
        pl.semaphore_signal(
            barrier, inc=1, device_id=(row, lax.rem(col + k, ncol)), device_id_type=MESH
        )
    for k in range(1, nrow):
        pl.semaphore_signal(
            barrier, inc=1, device_id=(lax.rem(row + k, nrow), col), device_id_type=MESH
        )
    pl.semaphore_wait(barrier, ncol + nrow - 2)


def dot(a, b):
    return jnp.dot(a, b, preferred_element_type=F32)


def dot_nt(a, b):
    return lax.dot_general(a, b, (((1,), (1,)), ((), ())), preferred_element_type=F32)


def main_kernel(
    nrow, ncol, wt, pair, q, k_in, v, d,
    f_out, wb_out, q_out, k_out, v_out,
    pv, bias, e_buf, g_buf, qd, kv, qd_all, kv_all, qt, dt, kt, vt,
    st, got, back, bk, dq, dq_near, dq_far, dkv, dkv_near, dkv_far,
    acc, wb, w1, w1sum, w2, w2sum, f_st,
    psem, up_s, down_s, zr, fs, fr, ks, kr, js, jr, s1, r1, s2, r2,
    qn_s, qn_r, qf_s, qf_r, gn_s, gn_r, gf_s, gf_r,
    ws1, wr1, ws2, wr2, ws3, wr3, ws4, wr4, fsem,
):
    row, col = lax.axis_index("row"), lax.axis_index("col")
    R, C, W = pair.shape
    H = wt.shape[0]
    Cp = pv.shape[1]
    hb, hr = H // ncol, H // nrow
    dcol, drow = hb * HD, hr * HD
    wr = W // nrow
    chunks = R // STEP
    inner, outer, rin, rout = split(ncol) + split(nrow)
    a, b_in = col // inner, lax.rem(col, inner)
    flip = a * inner + inner - 1 - b_in
    x_at, core = row // rin, lax.rem(row, rin)
    twin = x_at * rin + rin - 1 - core
    upper_half = (2 * a) // outer
    slot = b_in * outer + (1 - upper_half) * 2 * a + upper_half * (2 * (outer - a) - 1)

    def block_at(p):
        q = lax.rem(p, outer)
        odd = lax.rem(q, 2)
        end = (1 - odd) * (q // 2) + odd * (outer - 1 - q // 2)
        return end * inner + p // outer

    folded, half = folds(R, hb)
    main_lanes = LANES if folded else R

    def put_row(ref, b, s, n, x):
        ref[b, s:s + 1, :] = x[:, :main_lanes]
        if folded:
            at = (s % 2) * half
            ref[b, n + s // 2:n + s // 2 + 1, at:at + half] = x[:, main_lanes:]

    def get_row(ref, b, s, n):
        x = ref[b, s:s + 1, :]
        if folded:
            at = (s % 2) * half
            tail = ref[b, n + s // 2:n + s // 2 + 1, at:at + half]
            x = jnp.concatenate([x, tail], axis=1)
        return x

    def load(t):
        rows = pl.ds(t * STEP, STEP)
        return pltpu.make_async_copy(pair.at[rows], pv.at[rows, pl.ds(0, C)], psem.at[t])

    @pl.loop(0, chunks)
    def _(t):
        load(t).start()

    qd_own = jnp.concatenate([q[...], d[...]], axis=1)
    kv_own = jnp.concatenate([k_in[...], v[...]], axis=1)
    qd[...] = qd_own
    kv[...] = kv_own
    qd_all[col] = qd_own
    kv_all[row] = kv_own
    greet(nrow, ncol, row, col)

    def line(src):
        return src * inner + b_in

    def pass_up(src, ref):
        return remote(ref, qd_all.at[line(src)], up_s.at[src], zr.at[src], row, col + inner)

    def pass_down(src, ref):
        return remote(ref, qd_all.at[line(src)], down_s.at[src], zr.at[src], row, col - inner)

    def pass_flip(src, ref):
        return remote(ref, qd_all.at[line(src)], fs.at[src], fr.at[src], row, flip)

    @pl.when(a + 1 < outer)
    def _():
        pass_up(a, qd).start()

    @pl.when(a > 0)
    def _():
        pass_down(a, qd).start()

    if inner == 2:
        pass_flip(a, qd).start()

    def kv_far(k):
        to = lax.rem(x_at + k, rout) * rin + core
        return remote(kv, kv_all.at[row], ks.at[k], kr.at[k], to, col)

    def kv_twin(k, ref):
        src = lax.rem(x_at + rout - k, rout) * rin + core
        return remote(ref, kv_all.at[src], js.at[k], jr.at[k], twin, col)

    for k in range(1, rout):
        kv_far(k).start()
    if rin == 2:
        kv_twin(0, kv).start()

    def arrive(j):
        @pl.when(a >= j)
        def _():
            src = a - j
            here = qd_all.at[line(src)]
            pass_up(src, here).wait_recv()

            @pl.when(a + 1 < outer)
            def _():
                pass_up(src, here).start()

            if inner == 2:
                pass_flip(src, here).start()

        @pl.when(a + j < outer)
        def _():
            src = a + j
            here = qd_all.at[line(src)]
            pass_down(src, here).wait_recv()

            @pl.when(a > 0)
            def _():
                pass_down(src, here).start()

            if inner == 2:
                pass_flip(src, here).start()

    def kv_arrive(k):
        src = lax.rem(x_at + rout - k, rout) * rin + core
        remote(kv, kv_all.at[src], ks.at[k], kr.at[k], row, col).wait_recv()
        if rin == 2:
            kv_twin(k, kv_all.at[src]).start()

    if Cp > C:
        pv[:, C:, :] = jnp.zeros((R, Cp - C, W), BF16)

    @pl.loop(0, chunks)
    def _(t):
        load(t).wait()
        for u in range(0, STEP, 2):
            i = t * STEP + u
            r = dot_nt(wt[...], pv[pl.ds(i, 2)].reshape(2 * Cp, W))
            bias[pl.ds(i, H, stride=R), :] = r[:, :Cp]
            bias[pl.ds(i + 1, H, stride=R), :] = r[:, Cp:]
        for j in range(1, outer):
            if HOP * j < chunks:

                @pl.when(t == HOP * j - 1)
                def _():
                    arrive(j)

        if HOP < chunks:

            @pl.when(t == HOP)
            def _():
                for k in range(1, rout):
                    kv_arrive(k)

    if HOP >= chunks:
        for k in range(1, rout):
            kv_arrive(k)
    for j in range(1, outer):
        if HOP * j >= chunks:
            arrive(j)
    if rin == 2:
        for k in range(rout):
            src = lax.rem(x_at + rout - k, rout) * rin + rin - 1 - core
            remote(kv, kv_all.at[src], js.at[k], jr.at[k], row, col).wait_recv()

    @pl.loop(0, nrow)
    def _(r):
        x = kv_all[r].T
        kt[pl.ds(r * hr, hr)] = x[:drow].reshape(hr, HD, C)
        vt[pl.ds(r * hr, hr)] = x[drow:].reshape(hr, HD, C)

    lag = ncol // 2

    def combine():
        for k in range(1, ncol):
            src = lax.rem(col + k, ncol)
            remote(st.at[src], got.at[src], s1.at[src], r1.at[src], row, col).wait_recv()
        got[col] = st[col]
        sections = [(0, 0, hb)]
        if folded:
            sections.append((3 * hb, 2 * hb, hb // 2))
        for lo, out, n in sections:
            top = got[0, lo:lo + n]
            for k in range(1, ncol):
                top = jnp.maximum(top, got[k, lo:lo + n])
            total = jnp.zeros_like(top)
            upper = jnp.zeros_like(top)
            for k in range(ncol):
                scale = jnp.exp(got[k, lo:lo + n] - top)
                total += got[k, lo + n:lo + 2 * n] * scale
                upper += got[k, lo + 2 * n:lo + 3 * n] * scale
            delta = upper / total
            for k in range(ncol):
                back[k, out:out + n] = jnp.exp(got[k, lo:lo + n] - top) / total
                back[k, out + n:out + 2 * n] = delta
        bk[col] = back[col]
        for k in range(1, ncol):
            to = lax.rem(col + k, ncol)
            remote(back.at[to], bk.at[col], s2.at[to], r2.at[col], row, to).start()

    @pl.loop(0, ncol)
    def _(p):
        b = block_at(p)
        if inner == 2:

            @pl.when(lax.rem(b, inner) != b_in)
            def _():
                at = b // inner
                remote(qd, qd_all.at[b], fs.at[at], fr.at[at], row, col).wait_recv()

        x = qd_all[b].T
        qt[pl.ds(b * hb, hb)] = (x[:dcol] * jnp.asarray(SCALE, BF16)).reshape(hb, HD, R)
        dt[pl.ds(b * hb, hb)] = x[dcol:].reshape(hb, HD, R)
        heads = pl.ds(b * hb, hb)
        kb = kt[heads].reshape(dcol, C).T
        vb = vt[heads].reshape(dcol, C).T
        qb = qt[heads].reshape(dcol, R)
        db = dt[heads].reshape(dcol, R)
        owner = lax.broadcasted_iota(jnp.int32, (C, dcol), 1) // HD
        zero = jnp.zeros((C, dcol), BF16)
        for t in range(hb):
            h = b * hb + t
            term = bias[pl.ds(pl.multiple_of(h * R, 8), R), :].T[:C]
            s = dot(jnp.where(owner == t, kb, zero), qb) + term
            g = dot(jnp.where(owner == t, vb, zero), db)
            top = jnp.max(s, axis=0, keepdims=True)
            e = jnp.exp(s - top)
            e_buf[h] = e
            g_buf[h] = g
            put_row(st, b, t, 3 * hb, top)
            put_row(st, b, hb + t, 3 * hb, jnp.sum(e, axis=0, keepdims=True))
            put_row(st, b, 2 * hb + t, 3 * hb, jnp.sum(e * g, axis=0, keepdims=True))

        @pl.when(col != b)
        def _():
            remote(st.at[b], got.at[col], s1.at[b], r1.at[col], row, b).start()

        @pl.when(slot == p - lag)
        def _():
            combine()

    def send_dkv(r):
        at = r // rin
        return remote(dkv.at[r], dkv_near.at[at], gn_s.at[at], gn_r.at[at], twin, col)

    def send_dq(b):
        at = b // inner
        return remote(dq.at[b], dq_near.at[at], qn_s.at[at], qn_r.at[at], row, flip)

    @pl.loop(0, ncol)
    def _(p):
        b = block_at(p)

        @pl.when(slot == ncol - lag + p)
        def _():
            combine()

        @pl.when(col != b)
        def _():
            remote(back.at[b], bk.at[b], s2.at[b], r2.at[b], row, col).wait_recv()

        for t in range(hb):
            h = b * hb + t
            r = h // hr
            w = e_buf[h] * get_row(bk, b, t, 2 * hb)
            ds = (w * (g_buf[h] - get_row(bk, b, hb + t, 2 * hb))).astype(BF16)
            low = w.astype(BF16)
            y = (dot(kt[h], ds) * SCALE).astype(BF16)
            dq[b, t * HD:(t + 1) * HD, :] = y[:, :main_lanes]
            if folded:
                lo, at = dcol + (t // 2) * HD, (t % 2) * half
                dq[b, lo:lo + HD, at:at + half] = y[:, main_lanes:]
            dkv[r, 0, lax.rem(h, hr)] = dot_nt(qt[h], ds).astype(BF16)
            dkv[r, 1, lax.rem(h, hr)] = dot_nt(dt[h], low).astype(BF16)
            bias[pl.ds(pl.multiple_of(h * R, 8), R), pl.ds(0, C)] = ds.astype(F32).T

        if inner == 2:

            @pl.when(lax.rem(b, inner) != b_in)
            def _():
                send_dq(b).start()

    if rin == 2:
        for x in range(rout):
            send_dkv(x * rin + rin - 1 - core).start()

    def merge_dq(at):
        value = dq[at * inner + b_in].astype(F32)
        if inner == 2:
            remote(dq.at[0], dq_near.at[at], qn_s.at[0], qn_r.at[at], row, col).wait_recv()
            value += dq_near[at].astype(F32)
        return value

    def merge_dkv(at):
        value = dkv[at * rin + core].astype(F32)
        if rin == 2:
            remote(dkv.at[0], dkv_near.at[at], gn_s.at[0], gn_r.at[at], row, col).wait_recv()
            value += dkv_near[at].astype(F32)
        return value

    def far_dq(at):
        to = at * inner + b_in
        return remote(dq.at[to], dq_far.at[a], qf_s.at[at], qf_r.at[a], row, to)

    def far_dkv(at):
        to = at * rin + core
        return remote(dkv.at[to], dkv_far.at[x_at], gf_s.at[at], gf_r.at[x_at], to, col)

    def merge():
        for k in range(1, outer):
            at = lax.rem(a + k, outer)
            dq[at * inner + b_in] = merge_dq(at).astype(BF16)
            far_dq(at).start()
        for k in range(1, rout):
            at = lax.rem(x_at + k, rout)
            dkv[at * rin + core] = merge_dkv(at).astype(BF16)
            far_dkv(at).start()

    acc[...] = jnp.zeros_like(acc)

    def rows_of(i):
        return bias[pl.ds(i, H, stride=R), :]

    wide = 2 * STEP if R % (4 * STEP) == 0 else STEP
    laps = R // wide

    def weight(t):
        total = acc[...]
        for u in range(0, wide, 2):
            i = t * wide + u
            lhs = jnp.concatenate(
                [rows_of(i).astype(BF16), rows_of(i + 1).astype(BF16)], axis=1
            )
            total = total + dot(lhs, pv[pl.ds(i, 2)].reshape(2 * Cp, W))
        acc[...] = total

    pl.loop(0, laps // 2)(weight)
    merge()
    pl.loop(laps // 2, laps)(weight)

    for r in range(nrow):
        for b in range(ncol):
            wb[r, b] = acc[b * hb:(b + 1) * hb, r * wr:(r + 1) * wr].astype(BF16)

    def put(t, slot):
        return pltpu.make_async_copy(
            f_st.at[slot], f_out.at[pl.ds(t * STEP, STEP)], fsem.at[slot]
        )

    def flat(lo, hi):
        @pl.loop(lo, hi)
        def _(t):
            slot = lax.rem(t, SLOTS)

            @pl.when(t >= SLOTS)
            def _():
                put(t - SLOTS, slot).wait()

            for u in range(STEP):
                f_st[slot, u] = rows_of(t * STEP + u).T[:C].astype(BF16)
            put(t, slot).start()

    cuts = [0, chunks // 4, (2 * chunks) // 3, chunks - chunks // 8, chunks]

    for k in range(1, nrow):
        to = lax.rem(row + k, nrow)
        remote(wb.at[to], w1.at[k], ws1.at[k], wr1.at[k], to, col).start()
    flat(cuts[0], cuts[1])
    total = wb[row].astype(F32)
    for k in range(1, nrow):
        remote(wb.at[0], w1.at[k], ws1.at[k], wr1.at[k], row, col).wait_recv()
        total += w1[k].astype(F32)
    w1sum[...] = total
    for k in range(1, ncol):
        to = lax.rem(col + k, ncol)
        remote(w1sum.at[to], w2.at[k], ws2.at[k], wr2.at[k], row, to).start()
    flat(cuts[1], cuts[2])
    part = w1sum[col]
    for k in range(1, ncol):
        remote(w1sum.at[0], w2.at[k], ws2.at[k], wr2.at[k], row, col).wait_recv()
        part += w2[k]
    part = part.astype(BF16)
    w2sum[...] = part
    wb_out[row, col] = part
    for k in range(1, ncol):
        to = lax.rem(col + k, ncol)
        remote(w2sum, wb_out.at[row, col], ws3.at[k], wr3.at[k], row, to).start()
    flat(cuts[2], cuts[3])

    grad = merge_dkv(x_at)
    for k in range(1, rout):
        src = lax.rem(x_at + k, rout)
        remote(dkv.at[0], dkv_far.at[src], gf_s.at[0], gf_r.at[src], row, col).wait_recv()
        grad += dkv_far[src].astype(F32)
    k_out[...] = grad[0].reshape(drow, C).T.astype(BF16)
    v_out[...] = grad[1].reshape(drow, C).T.astype(BF16)
    grad = merge_dq(a)
    for k in range(1, outer):
        src = lax.rem(a + k, outer)
        remote(dq.at[0], dq_far.at[src], qf_s.at[0], qf_r.at[src], row, col).wait_recv()
        grad += dq_far[src].astype(F32)
    if folded:
        tail = grad[dcol:].reshape(hb // 2, HD, LANES)
        tail = jnp.stack([tail[:, :, :half], tail[:, :, half:]], axis=1).reshape(dcol, half)
        q_out[:LANES] = grad[:dcol].T.astype(BF16)
        q_out[LANES:] = tail.T.astype(BF16)
    else:
        q_out[...] = grad.T.astype(BF16)

    for k in range(1, ncol):
        src = lax.rem(col + ncol - k, ncol)
        remote(w2sum, wb_out.at[row, src], ws3.at[k], wr3.at[k], row, col).wait_recv()
    for k in range(1, nrow):
        to = lax.rem(row + k, nrow)
        remote(wb_out.at[row], wb_out.at[row], ws4.at[k], wr4.at[k], to, col).start()
    flat(cuts[3], cuts[4])
    for k in range(1, nrow):
        src = lax.rem(row + nrow - k, nrow)
        remote(wb_out.at[src], wb_out.at[src], ws4.at[k], wr4.at[k], row, col).wait_recv()

    for t in range(max(0, chunks - SLOTS), chunks):
        put(t, t % SLOTS).wait()
    for src in range(outer):

        @pl.when(jnp.logical_and(a >= src, a + 1 < outer))
        def _():
            pass_up(src, qd).wait_send()

        @pl.when(jnp.logical_and(a <= src, a > 0))
        def _():
            pass_down(src, qd).wait_send()

        if inner == 2:
            pass_flip(src, qd).wait_send()
            send_dq(src * inner + 1 - b_in).wait_send()
    for k in range(rout):
        if rin == 2:
            kv_twin(k, kv).wait_send()
            send_dkv(k * rin + 1 - core).wait_send()
        if k:
            kv_far(k).wait_send()
            far_dkv(lax.rem(x_at + k, rout)).wait_send()
    for k in range(1, outer):
        far_dq(lax.rem(a + k, outer)).wait_send()
    for k in range(1, ncol):
        to = lax.rem(col + k, ncol)
        remote(st.at[to], got.at[col], s1.at[to], r1.at[col], row, to).wait_send()
        remote(back.at[to], bk.at[col], s2.at[to], r2.at[col], row, to).wait_send()
        remote(w1sum.at[to], w2.at[k], ws2.at[k], wr2.at[k], row, to).wait_send()
        remote(w2sum, wb_out.at[row, col], ws3.at[k], wr3.at[k], row, to).wait_send()
    for k in range(1, nrow):
        to = lax.rem(row + k, nrow)
        remote(wb.at[to], w1.at[k], ws1.at[k], wr1.at[k], to, col).wait_send()
        remote(wb_out.at[row], wb_out.at[row], ws4.at[k], wr4.at[k], to, col).wait_send()


def main(nrow, ncol, wt, pair, q, k, v, d):
    R, C, W = pair.shape
    H = wt.shape[0]
    hb, hr = H // ncol, H // nrow
    dcol, drow = q.shape[1], k.shape[1]
    Cp = -(-C // LANES) * LANES
    wr = W // nrow
    shape = jax.ShapeDtypeStruct
    (inner, outer), (rin, rout) = split(ncol), split(nrow)
    folded, _ = folds(R, hb)
    width = LANES if folded else R
    extra = 3 * hb // 2 if folded else 0
    dq_rows = dcol + (dcol // 2 if folded else 0)
    return pl.pallas_call(
        functools.partial(main_kernel, nrow, ncol),
        out_shape=(
            shape((R, C, H), BF16),
            shape((nrow, ncol, hb, wr), BF16),
            shape((R, dcol), BF16),
            shape((C, drow), BF16),
            shape((C, drow), BF16),
        ),
        in_specs=[pl.BlockSpec(memory_space=VMEM), pl.BlockSpec(memory_space=pl.ANY)]
        + [pl.BlockSpec(memory_space=VMEM)] * 4,
        out_specs=[pl.BlockSpec(memory_space=pl.ANY)] + [pl.BlockSpec(memory_space=VMEM)] * 4,
        scratch_shapes=[
            VMEM((R, Cp, W), BF16),
            VMEM((H * R, Cp), F32),
            VMEM((H, C, R), F32),
            VMEM((H, C, R), F32),
            VMEM((R, 2 * dcol), BF16),
            VMEM((C, 2 * drow), BF16),
            VMEM((ncol, R, 2 * dcol), BF16),
            VMEM((nrow, C, 2 * drow), BF16),
            VMEM((H, HD, R), BF16),
            VMEM((H, HD, R), BF16),
            VMEM((H, HD, C), BF16),
            VMEM((H, HD, C), BF16),
            VMEM((ncol, 3 * hb + extra, width), F32),
            VMEM((ncol, 3 * hb + extra, width), F32),
            VMEM((ncol, 2 * hb + (hb if folded else 0), width), F32),
            VMEM((ncol, 2 * hb + (hb if folded else 0), width), F32),
            VMEM((ncol, dq_rows, width), BF16),
            VMEM((outer, dq_rows, width), BF16),
            VMEM((outer, dq_rows, width), BF16),
            VMEM((nrow, 2, hr, HD, C), BF16),
            VMEM((rout, 2, hr, HD, C), BF16),
            VMEM((rout, 2, hr, HD, C), BF16),
            VMEM((H, W), F32),
            VMEM((nrow, ncol, hb, wr), BF16),
            VMEM((nrow, ncol, hb, wr), BF16),
            VMEM((ncol, hb, wr), F32),
            VMEM((ncol, hb, wr), F32),
            VMEM((hb, wr), BF16),
            VMEM((SLOTS, STEP, C, H), BF16),
            DMA((R // STEP,)),
            DMA((outer,)), DMA((outer,)), DMA((outer,)), DMA((outer,)), DMA((outer,)),
            DMA((rout,)), DMA((rout,)), DMA((rout,)), DMA((rout,)),
            DMA((ncol,)), DMA((ncol,)), DMA((ncol,)), DMA((ncol,)),
            DMA((outer,)), DMA((outer,)), DMA((outer,)), DMA((outer,)),
            DMA((rout,)), DMA((rout,)), DMA((rout,)), DMA((rout,)),
            DMA((nrow,)), DMA((nrow,)), DMA((ncol,)), DMA((ncol,)),
            DMA((ncol,)), DMA((ncol,)), DMA((nrow,)), DMA((nrow,)),
            DMA((SLOTS,)),
        ],
        compiler_params=pltpu.CompilerParams(
            collective_id=0, has_side_effects=True, vmem_limit_bytes=67043328
        ),
    )(wt, pair, q, k, v, d)


def finish_kernel(
    f, wt, wb, q, k, v, d_pair, wo, qo, ko, vo, f_all, stage, w_all, fsem, osem, ssem
):
    R, C, H = f.shape
    laps = R // STEP
    slots = stage.shape[0]

    def fetch(t):
        rows = pl.ds(t * STEP, STEP)
        return pltpu.make_async_copy(f.at[rows], f_all.at[rows], fsem.at[t])

    def put(t, slot):
        rows = pl.ds(t * STEP, STEP)
        return pltpu.make_async_copy(stage.at[slot], d_pair.at[rows], osem.at[slot])

    @pl.loop(0, laps)
    def _(t):
        fetch(t).start()

    nrow, wr = wb.shape[0], wb.shape[3]
    for r in range(nrow):
        w_all[:, r * wr:(r + 1) * wr] = wb[r].astype(F32).reshape(H, wr)
    small = [
        pltpu.make_async_copy(src, dst, ssem.at[n])
        for n, (src, dst) in enumerate([(w_all, wo), (q, qo), (k, ko), (v, vo)])
    ]
    for copy in small:
        copy.start()

    @pl.loop(0, laps)
    def _(t):
        slot = lax.rem(t, slots)
        fetch(t).wait()

        @pl.when(t >= slots)
        def _():
            put(t - slots, slot).wait()

        lhs = f_all[pl.ds(t * STEP, STEP)].reshape(STEP * C, H)
        stage[slot] = dot(lhs, wt[...]).astype(BF16).reshape(STEP, C, stage.shape[3])
        put(t, slot).start()

    for t in range(max(0, laps - slots), laps):
        put(t, t % slots).wait()
    for copy in small:
        copy.wait()


def finish(f, wt, wb, q, k, v):
    R, C, H = f.shape
    W = wt.shape[1]
    laps = R // STEP
    slots = min(4, laps)
    return pl.pallas_call(
        finish_kernel,
        out_shape=(
            jax.ShapeDtypeStruct((R, C, W), BF16),
            jax.ShapeDtypeStruct((H, W), F32),
            jax.ShapeDtypeStruct(q.shape, BF16),
            jax.ShapeDtypeStruct(k.shape, BF16),
            jax.ShapeDtypeStruct(v.shape, BF16),
        ),
        in_specs=[pl.BlockSpec(memory_space=pl.ANY)] + [pl.BlockSpec(memory_space=VMEM)] * 5,
        out_specs=[pl.BlockSpec(memory_space=pl.ANY)] * 5,
        scratch_shapes=[
            VMEM((R, C, H), BF16),
            VMEM((slots, STEP, C, W), BF16),
            VMEM((H, W), F32),
            DMA((laps,)),
            DMA((slots,)),
            DMA((4,)),
        ],
        compiler_params=pltpu.CompilerParams(vmem_limit_bytes=67043328),
    )(f, wt, wb, q, k, v)


def on_device(nrow, ncol, pair, w_bias, queries, keys, values, d_out):
    wt = w_bias.T
    f, wb, q, k, v = main(nrow, ncol, wt, pair, queries, keys, values, d_out)
    d_pair, d_wbias, d_queries, d_keys, d_values = finish(f, wt, wb, q, k, v)
    return d_pair, d_wbias.T, d_queries, d_keys, d_values


def solution(mesh):
    return jax.shard_map(
        functools.partial(on_device, mesh.shape["row"], mesh.shape["col"]),
        mesh=mesh,
        in_specs=(
            P("row", "col", None),
            P(),
            P("row", "col"),
            P("col", "row"),
            P("col", "row"),
            P("row", "col"),
        ),
        out_specs=(P("row", "col", None), P(), P("row", "col"), P("col", "row"), P("col", "row")),
        check_vma=False,
    )
```

```python
import functools

import jax
import jax.numpy as jnp
from jax import lax
from jax.experimental import pallas as pl
from jax.experimental.pallas import tpu as pltpu
from jax.sharding import PartitionSpec as P

HD = 16
SCALE = 1.0 / HD**0.5
LANES = 128
STEP = 16
SLOTS = 2
HOP = 4
MESH = pl.DeviceIdType.MESH
VMEM = pltpu.VMEM
DMA = pltpu.SemaphoreType.DMA
F32 = jnp.float32
BF16 = jnp.bfloat16


def remote(src, dst, send, recv, row, col):
    return pltpu.make_async_remote_copy(
        src_ref=src, dst_ref=dst, send_sem=send, recv_sem=recv,
        device_id=(row, col), device_id_type=MESH,
    )


def split(n):
    return (2, n // 2) if n % 2 == 0 else (1, n)


def folds(R, hb):
    half = R % LANES
    return R == LANES + half and 2 * half == LANES and hb % 2 == 0, half


def greet(nrow, ncol, row, col):
    barrier = pltpu.get_barrier_semaphore()
    for k in range(1, ncol):
        pl.semaphore_signal(
            barrier, inc=1, device_id=(row, lax.rem(col + k, ncol)), device_id_type=MESH
        )
    for k in range(1, nrow):
        pl.semaphore_signal(
            barrier, inc=1, device_id=(lax.rem(row + k, nrow), col), device_id_type=MESH
        )
    pl.semaphore_wait(barrier, ncol + nrow - 2)


def dot(a, b):
    return jnp.dot(a, b, preferred_element_type=F32)


def dot_nt(a, b):
    return lax.dot_general(a, b, (((1,), (1,)), ((), ())), preferred_element_type=F32)


def main_kernel(
    nrow, ncol, wt, pair, q, k_in, v, d,
    f_out, wb_out, q_out, k_out, v_out,
    pv, bias, e_buf, g_buf, qd, kv, qd_all, kv_all, qt, dt, kt, vt,
    st, got, back, bk, dq, dq_near, dq_far, dkv, dkv_near, dkv_far,
    acc, wb, w1, w1sum, w2, w2sum, f_st,
    psem, up_s, down_s, zr, fs, fr, ks, kr, js, jr, s1, r1, s2, r2,
    qn_s, qn_r, qf_s, qf_r, gn_s, gn_r, gf_s, gf_r,
    ws1, wr1, ws2, wr2, ws3, wr3, ws4, wr4, fsem,
):
    row, col = lax.axis_index("row"), lax.axis_index("col")
    R, C, W = pair.shape
    H = wt.shape[0]
    Cp = pv.shape[1]
    hb, hr = H // ncol, H // nrow
    dcol, drow = hb * HD, hr * HD
    wr = W // nrow
    chunks = R // STEP
    inner, outer, rin, rout = split(ncol) + split(nrow)
    a, b_in = col // inner, lax.rem(col, inner)
    flip = a * inner + inner - 1 - b_in
    x_at, core = row // rin, lax.rem(row, rin)
    twin = x_at * rin + rin - 1 - core
    upper_half = (2 * a) // outer
    slot = b_in * outer + (1 - upper_half) * 2 * a + upper_half * (2 * (outer - a) - 1)

    def block_at(p):
        q = lax.rem(p, outer)
        odd = lax.rem(q, 2)
        end = (1 - odd) * (q // 2) + odd * (outer - 1 - q // 2)
        return end * inner + p // outer

    folded, half = folds(R, hb)
    main_lanes = LANES if folded else R

    def put_row(ref, b, s, n, x):
        ref[b, s:s + 1, :] = x[:, :main_lanes]
        if folded:
            at = (s % 2) * half
            ref[b, n + s // 2:n + s // 2 + 1, at:at + half] = x[:, main_lanes:]

    def get_row(ref, b, s, n):
        x = ref[b, s:s + 1, :]
        if folded:
            at = (s % 2) * half
            tail = ref[b, n + s // 2:n + s // 2 + 1, at:at + half]
            x = jnp.concatenate([x, tail], axis=1)
        return x

    def load(t):
        rows = pl.ds(t * STEP, STEP)
        return pltpu.make_async_copy(pair.at[rows], pv.at[rows, pl.ds(0, C)], psem.at[t])

    @pl.loop(0, chunks)
    def _(t):
        load(t).start()

    qd_own = jnp.concatenate([q[...], d[...]], axis=1)
    kv_own = jnp.concatenate([k_in[...], v[...]], axis=1)
    qd[...] = qd_own
    kv[...] = kv_own
    qd_all[col] = qd_own
    kv_all[row] = kv_own
    greet(nrow, ncol, row, col)

    def line(src):
        return src * inner + b_in

    def pass_up(src, ref):
        return remote(ref, qd_all.at[line(src)], up_s.at[src], zr.at[src], row, col + inner)

    def pass_down(src, ref):
        return remote(ref, qd_all.at[line(src)], down_s.at[src], zr.at[src], row, col - inner)

    def pass_flip(src, ref):
        return remote(ref, qd_all.at[line(src)], fs.at[src], fr.at[src], row, flip)

    @pl.when(a + 1 < outer)
    def _():
        pass_up(a, qd).start()

    @pl.when(a > 0)
    def _():
        pass_down(a, qd).start()

    if inner == 2:
        pass_flip(a, qd).start()

    def kv_far(k):
        to = lax.rem(x_at + k, rout) * rin + core
        return remote(kv, kv_all.at[row], ks.at[k], kr.at[k], to, col)

    def kv_twin(k, ref):
        src = lax.rem(x_at + rout - k, rout) * rin + core
        return remote(ref, kv_all.at[src], js.at[k], jr.at[k], twin, col)

    for k in range(1, rout):
        kv_far(k).start()
    if rin == 2:
        kv_twin(0, kv).start()

    def arrive(j):
        @pl.when(a >= j)
        def _():
            src = a - j
            here = qd_all.at[line(src)]
            pass_up(src, here).wait_recv()

            @pl.when(a + 1 < outer)
            def _():
                pass_up(src, here).start()

            if inner == 2:
                pass_flip(src, here).start()

        @pl.when(a + j < outer)
        def _():
            src = a + j
            here = qd_all.at[line(src)]
            pass_down(src, here).wait_recv()

            @pl.when(a > 0)
            def _():
                pass_down(src, here).start()

            if inner == 2:
                pass_flip(src, here).start()

    def kv_arrive(k):
        src = lax.rem(x_at + rout - k, rout) * rin + core
        remote(kv, kv_all.at[src], ks.at[k], kr.at[k], row, col).wait_recv()
        if rin == 2:
            kv_twin(k, kv_all.at[src]).start()

    if Cp > C:
        pv[:, C:, :] = jnp.zeros((R, Cp - C, W), BF16)

    @pl.loop(0, chunks)
    def _(t):
        load(t).wait()
        for u in range(0, STEP, 2):
            i = t * STEP + u
            r = dot_nt(wt[...], pv[pl.ds(i, 2)].reshape(2 * Cp, W))
            bias[pl.ds(i, H, stride=R), :] = r[:, :Cp]
            bias[pl.ds(i + 1, H, stride=R), :] = r[:, Cp:]
        for j in range(1, outer):
            if HOP * j < chunks:

                @pl.when(t == HOP * j - 1)
                def _():
                    arrive(j)

        if HOP < chunks:

            @pl.when(t == HOP)
            def _():
                for k in range(1, rout):
                    kv_arrive(k)

    if HOP >= chunks:
        for k in range(1, rout):
            kv_arrive(k)
    for j in range(1, outer):
        if HOP * j >= chunks:
            arrive(j)
    if rin == 2:
        for k in range(rout):
            src = lax.rem(x_at + rout - k, rout) * rin + rin - 1 - core
            remote(kv, kv_all.at[src], js.at[k], jr.at[k], row, col).wait_recv()

    @pl.loop(0, nrow)
    def _(r):
        x = kv_all[r].T
        kt[pl.ds(r * hr, hr)] = x[:drow].reshape(hr, HD, C)
        vt[pl.ds(r * hr, hr)] = x[drow:].reshape(hr, HD, C)

    lag = min(ncol - 1, ncol // 2 + 1)

    def combine():
        for k in range(1, ncol):
            src = lax.rem(col + k, ncol)
            remote(st.at[src], got.at[src], s1.at[src], r1.at[src], row, col).wait_recv()
        got[col] = st[col]
        sections = [(0, 0, hb)]
        if folded:
            sections.append((3 * hb, 2 * hb, hb // 2))
        for lo, out, n in sections:
            top = got[0, lo:lo + n]
            for k in range(1, ncol):
                top = jnp.maximum(top, got[k, lo:lo + n])
            total = jnp.zeros_like(top)
            upper = jnp.zeros_like(top)
            for k in range(ncol):
                scale = jnp.exp(got[k, lo:lo + n] - top)
                total += got[k, lo + n:lo + 2 * n] * scale
                upper += got[k, lo + 2 * n:lo + 3 * n] * scale
            delta = upper / total
            for k in range(ncol):
                back[k, out:out + n] = jnp.exp(got[k, lo:lo + n] - top) / total
                back[k, out + n:out + 2 * n] = delta
        bk[col] = back[col]
        for k in range(1, ncol):
            to = lax.rem(col + k, ncol)
            remote(back.at[to], bk.at[col], s2.at[to], r2.at[col], row, to).start()

    @pl.loop(0, ncol)
    def _(p):
        b = block_at(p)
        if inner == 2:

            @pl.when(lax.rem(b, inner) != b_in)
            def _():
                at = b // inner
                remote(qd, qd_all.at[b], fs.at[at], fr.at[at], row, col).wait_recv()

        x = qd_all[b].T
        qt[pl.ds(b * hb, hb)] = (x[:dcol] * jnp.asarray(SCALE, BF16)).reshape(hb, HD, R)
        dt[pl.ds(b * hb, hb)] = x[dcol:].reshape(hb, HD, R)
        heads = pl.ds(b * hb, hb)
        kb = kt[heads].reshape(dcol, C).T
        vb = vt[heads].reshape(dcol, C).T
        qb = qt[heads].reshape(dcol, R)
        db = dt[heads].reshape(dcol, R)
        owner = lax.broadcasted_iota(jnp.int32, (C, dcol), 1) // HD
        zero = jnp.zeros((C, dcol), BF16)
        for t in range(hb):
            h = b * hb + t
            term = bias[pl.ds(pl.multiple_of(h * R, 8), R), :].T[:C]
            s = dot(jnp.where(owner == t, kb, zero), qb) + term
            g = dot(jnp.where(owner == t, vb, zero), db)
            top = jnp.max(s, axis=0, keepdims=True)
            e = jnp.exp(s - top)
            e_buf[h] = e
            g_buf[h] = g
            put_row(st, b, t, 3 * hb, top)
            put_row(st, b, hb + t, 3 * hb, jnp.sum(e, axis=0, keepdims=True))
            put_row(st, b, 2 * hb + t, 3 * hb, jnp.sum(e * g, axis=0, keepdims=True))

        @pl.when(col != b)
        def _():
            remote(st.at[b], got.at[col], s1.at[b], r1.at[col], row, b).start()

        @pl.when(slot == p - lag)
        def _():
            combine()

    def send_dkv(r):
        at = r // rin
        return remote(dkv.at[r], dkv_near.at[at], gn_s.at[at], gn_r.at[at], twin, col)

    def send_dq(b):
        at = b // inner
        return remote(dq.at[b], dq_near.at[at], qn_s.at[at], qn_r.at[at], row, flip)

    @pl.loop(0, ncol)
    def _(p):
        b = block_at(p)

        @pl.when(slot == ncol - lag + p)
        def _():
            combine()

        @pl.when(col != b)
        def _():
            remote(back.at[b], bk.at[b], s2.at[b], r2.at[b], row, col).wait_recv()

        for t in range(hb):
            h = b * hb + t
            r = h // hr
            w = e_buf[h] * get_row(bk, b, t, 2 * hb)
            ds = (w * (g_buf[h] - get_row(bk, b, hb + t, 2 * hb))).astype(BF16)
            low = w.astype(BF16)
            y = (dot(kt[h], ds) * SCALE).astype(BF16)
            dq[b, t * HD:(t + 1) * HD, :] = y[:, :main_lanes]
            if folded:
                lo, at = dcol + (t // 2) * HD, (t % 2) * half
                dq[b, lo:lo + HD, at:at + half] = y[:, main_lanes:]
            dkv[r, 0, lax.rem(h, hr)] = dot_nt(qt[h], ds).astype(BF16)
            dkv[r, 1, lax.rem(h, hr)] = dot_nt(dt[h], low).astype(BF16)
            bias[pl.ds(pl.multiple_of(h * R, 8), R), pl.ds(0, C)] = ds.astype(F32).T

        if inner == 2:

            @pl.when(lax.rem(b, inner) != b_in)
            def _():
                send_dq(b).start()

    if rin == 2:
        for x in range(rout):
            send_dkv(x * rin + rin - 1 - core).start()

    def merge_dq(at):
        value = dq[at * inner + b_in].astype(F32)
        if inner == 2:
            remote(dq.at[0], dq_near.at[at], qn_s.at[0], qn_r.at[at], row, col).wait_recv()
            value += dq_near[at].astype(F32)
        return value

    def merge_dkv(at):
        value = dkv[at * rin + core].astype(F32)
        if rin == 2:
            remote(dkv.at[0], dkv_near.at[at], gn_s.at[0], gn_r.at[at], row, col).wait_recv()
            value += dkv_near[at].astype(F32)
        return value

    def far_dq(at):
        to = at * inner + b_in
        return remote(dq.at[to], dq_far.at[a], qf_s.at[at], qf_r.at[a], row, to)

    def far_dkv(at):
        to = at * rin + core
        return remote(dkv.at[to], dkv_far.at[x_at], gf_s.at[at], gf_r.at[x_at], to, col)

    def merge():
        for k in range(1, outer):
            at = lax.rem(a + k, outer)
            dq[at * inner + b_in] = merge_dq(at).astype(BF16)
            far_dq(at).start()
        for k in range(1, rout):
            at = lax.rem(x_at + k, rout)
            dkv[at * rin + core] = merge_dkv(at).astype(BF16)
            far_dkv(at).start()

    acc[...] = jnp.zeros_like(acc)

    def rows_of(i):
        return bias[pl.ds(i, H, stride=R), :]

    wide = 2 * STEP if R % (4 * STEP) == 0 else STEP
    laps = R // wide

    def weight(t):
        total = acc[...]
        for u in range(0, wide, 2):
            i = t * wide + u
            lhs = jnp.concatenate(
                [rows_of(i).astype(BF16), rows_of(i + 1).astype(BF16)], axis=1
            )
            total = total + dot(lhs, pv[pl.ds(i, 2)].reshape(2 * Cp, W))
        acc[...] = total

    pl.loop(0, laps // 2)(weight)
    merge()
    pl.loop(laps // 2, laps)(weight)

    for r in range(nrow):
        for b in range(ncol):
            wb[r, b] = acc[b * hb:(b + 1) * hb, r * wr:(r + 1) * wr].astype(BF16)

    def put(t, slot):
        return pltpu.make_async_copy(
            f_st.at[slot], f_out.at[pl.ds(t * STEP, STEP)], fsem.at[slot]
        )

    def flat(lo, hi):
        @pl.loop(lo, hi)
        def _(t):
            slot = lax.rem(t, SLOTS)

            @pl.when(t >= SLOTS)
            def _():
                put(t - SLOTS, slot).wait()

            for u in range(STEP):
                f_st[slot, u] = rows_of(t * STEP + u).T[:C].astype(BF16)
            put(t, slot).start()

    cuts = [0, chunks // 4, (2 * chunks) // 3, chunks - chunks // 8, chunks]

    for k in range(1, nrow):
        to = lax.rem(row + k, nrow)
        remote(wb.at[to], w1.at[k], ws1.at[k], wr1.at[k], to, col).start()
    flat(cuts[0], cuts[1])
    total = wb[row].astype(F32)
    for k in range(1, nrow):
        remote(wb.at[0], w1.at[k], ws1.at[k], wr1.at[k], row, col).wait_recv()
        total += w1[k].astype(F32)
    w1sum[...] = total
    for k in range(1, ncol):
        to = lax.rem(col + k, ncol)
        remote(w1sum.at[to], w2.at[k], ws2.at[k], wr2.at[k], row, to).start()
    flat(cuts[1], cuts[2])
    part = w1sum[col]
    for k in range(1, ncol):
        remote(w1sum.at[0], w2.at[k], ws2.at[k], wr2.at[k], row, col).wait_recv()
        part += w2[k]
    part = part.astype(BF16)
    w2sum[...] = part
    wb_out[row, col] = part
    for k in range(1, ncol):
        to = lax.rem(col + k, ncol)
        remote(w2sum, wb_out.at[row, col], ws3.at[k], wr3.at[k], row, to).start()
    flat(cuts[2], cuts[3])

    grad = merge_dkv(x_at)
    for k in range(1, rout):
        src = lax.rem(x_at + k, rout)
        remote(dkv.at[0], dkv_far.at[src], gf_s.at[0], gf_r.at[src], row, col).wait_recv()
        grad += dkv_far[src].astype(F32)
    k_out[...] = grad[0].reshape(drow, C).T.astype(BF16)
    v_out[...] = grad[1].reshape(drow, C).T.astype(BF16)
    grad = merge_dq(a)
    for k in range(1, outer):
        src = lax.rem(a + k, outer)
        remote(dq.at[0], dq_far.at[src], qf_s.at[0], qf_r.at[src], row, col).wait_recv()
        grad += dq_far[src].astype(F32)
    if folded:
        tail = grad[dcol:].reshape(hb // 2, HD, LANES)
        tail = jnp.stack([tail[:, :, :half], tail[:, :, half:]], axis=1).reshape(dcol, half)
        q_out[:LANES] = grad[:dcol].T.astype(BF16)
        q_out[LANES:] = tail.T.astype(BF16)
    else:
        q_out[...] = grad.T.astype(BF16)

    for k in range(1, ncol):
        src = lax.rem(col + ncol - k, ncol)
        remote(w2sum, wb_out.at[row, src], ws3.at[k], wr3.at[k], row, col).wait_recv()
    for k in range(1, nrow):
        to = lax.rem(row + k, nrow)
        remote(wb_out.at[row], wb_out.at[row], ws4.at[k], wr4.at[k], to, col).start()
    flat(cuts[3], cuts[4])
    for k in range(1, nrow):
        src = lax.rem(row + nrow - k, nrow)
        remote(wb_out.at[src], wb_out.at[src], ws4.at[k], wr4.at[k], row, col).wait_recv()

    for t in range(max(0, chunks - SLOTS), chunks):
        put(t, t % SLOTS).wait()
    for src in range(outer):

        @pl.when(jnp.logical_and(a >= src, a + 1 < outer))
        def _():
            pass_up(src, qd).wait_send()

        @pl.when(jnp.logical_and(a <= src, a > 0))
        def _():
            pass_down(src, qd).wait_send()

        if inner == 2:
            pass_flip(src, qd).wait_send()
            send_dq(src * inner + 1 - b_in).wait_send()
    for k in range(rout):
        if rin == 2:
            kv_twin(k, kv).wait_send()
            send_dkv(k * rin + 1 - core).wait_send()
        if k:
            kv_far(k).wait_send()
            far_dkv(lax.rem(x_at + k, rout)).wait_send()
    for k in range(1, outer):
        far_dq(lax.rem(a + k, outer)).wait_send()
    for k in range(1, ncol):
        to = lax.rem(col + k, ncol)
        remote(st.at[to], got.at[col], s1.at[to], r1.at[col], row, to).wait_send()
        remote(back.at[to], bk.at[col], s2.at[to], r2.at[col], row, to).wait_send()
        remote(w1sum.at[to], w2.at[k], ws2.at[k], wr2.at[k], row, to).wait_send()
        remote(w2sum, wb_out.at[row, col], ws3.at[k], wr3.at[k], row, to).wait_send()
    for k in range(1, nrow):
        to = lax.rem(row + k, nrow)
        remote(wb.at[to], w1.at[k], ws1.at[k], wr1.at[k], to, col).wait_send()
        remote(wb_out.at[row], wb_out.at[row], ws4.at[k], wr4.at[k], to, col).wait_send()


def main(nrow, ncol, wt, pair, q, k, v, d):
    R, C, W = pair.shape
    H = wt.shape[0]
    hb, hr = H // ncol, H // nrow
    dcol, drow = q.shape[1], k.shape[1]
    Cp = -(-C // LANES) * LANES
    wr = W // nrow
    shape = jax.ShapeDtypeStruct
    (inner, outer), (rin, rout) = split(ncol), split(nrow)
    folded, _ = folds(R, hb)
    width = LANES if folded else R
    extra = 3 * hb // 2 if folded else 0
    dq_rows = dcol + (dcol // 2 if folded else 0)
    return pl.pallas_call(
        functools.partial(main_kernel, nrow, ncol),
        out_shape=(
            shape((R, C, H), BF16),
            shape((nrow, ncol, hb, wr), BF16),
            shape((R, dcol), BF16),
            shape((C, drow), BF16),
            shape((C, drow), BF16),
        ),
        in_specs=[pl.BlockSpec(memory_space=VMEM), pl.BlockSpec(memory_space=pl.ANY)]
        + [pl.BlockSpec(memory_space=VMEM)] * 4,
        out_specs=[pl.BlockSpec(memory_space=pl.ANY)] + [pl.BlockSpec(memory_space=VMEM)] * 4,
        scratch_shapes=[
            VMEM((R, Cp, W), BF16),
            VMEM((H * R, Cp), F32),
            VMEM((H, C, R), F32),
            VMEM((H, C, R), F32),
            VMEM((R, 2 * dcol), BF16),
            VMEM((C, 2 * drow), BF16),
            VMEM((ncol, R, 2 * dcol), BF16),
            VMEM((nrow, C, 2 * drow), BF16),
            VMEM((H, HD, R), BF16),
            VMEM((H, HD, R), BF16),
            VMEM((H, HD, C), BF16),
            VMEM((H, HD, C), BF16),
            VMEM((ncol, 3 * hb + extra, width), F32),
            VMEM((ncol, 3 * hb + extra, width), F32),
            VMEM((ncol, 2 * hb + (hb if folded else 0), width), F32),
            VMEM((ncol, 2 * hb + (hb if folded else 0), width), F32),
            VMEM((ncol, dq_rows, width), BF16),
            VMEM((outer, dq_rows, width), BF16),
            VMEM((outer, dq_rows, width), BF16),
            VMEM((nrow, 2, hr, HD, C), BF16),
            VMEM((rout, 2, hr, HD, C), BF16),
            VMEM((rout, 2, hr, HD, C), BF16),
            VMEM((H, W), F32),
            VMEM((nrow, ncol, hb, wr), BF16),
            VMEM((nrow, ncol, hb, wr), BF16),
            VMEM((ncol, hb, wr), F32),
            VMEM((ncol, hb, wr), F32),
            VMEM((hb, wr), BF16),
            VMEM((SLOTS, STEP, C, H), BF16),
            DMA((R // STEP,)),
            DMA((outer,)), DMA((outer,)), DMA((outer,)), DMA((outer,)), DMA((outer,)),
            DMA((rout,)), DMA((rout,)), DMA((rout,)), DMA((rout,)),
            DMA((ncol,)), DMA((ncol,)), DMA((ncol,)), DMA((ncol,)),
            DMA((outer,)), DMA((outer,)), DMA((outer,)), DMA((outer,)),
            DMA((rout,)), DMA((rout,)), DMA((rout,)), DMA((rout,)),
            DMA((nrow,)), DMA((nrow,)), DMA((ncol,)), DMA((ncol,)),
            DMA((ncol,)), DMA((ncol,)), DMA((nrow,)), DMA((nrow,)),
            DMA((SLOTS,)),
        ],
        compiler_params=pltpu.CompilerParams(
            collective_id=0, has_side_effects=True, vmem_limit_bytes=67043328
        ),
    )(wt, pair, q, k, v, d)


def finish_kernel(
    f, wt, wb, q, k, v, d_pair, wo, qo, ko, vo, f_all, stage, w_all, fsem, osem, ssem
):
    R, C, H = f.shape
    laps = R // STEP
    slots = stage.shape[0]

    def fetch(t):
        rows = pl.ds(t * STEP, STEP)
        return pltpu.make_async_copy(f.at[rows], f_all.at[rows], fsem.at[t])

    def put(t, slot):
        rows = pl.ds(t * STEP, STEP)
        return pltpu.make_async_copy(stage.at[slot], d_pair.at[rows], osem.at[slot])

    @pl.loop(0, laps)
    def _(t):
        fetch(t).start()

    nrow, wr = wb.shape[0], wb.shape[3]
    for r in range(nrow):
        w_all[:, r * wr:(r + 1) * wr] = wb[r].astype(F32).reshape(H, wr)
    small = [
        pltpu.make_async_copy(src, dst, ssem.at[n])
        for n, (src, dst) in enumerate([(w_all, wo), (q, qo), (k, ko), (v, vo)])
    ]
    for copy in small:
        copy.start()

    @pl.loop(0, laps)
    def _(t):
        slot = lax.rem(t, slots)
        fetch(t).wait()

        @pl.when(t >= slots)
        def _():
            put(t - slots, slot).wait()

        lhs = f_all[pl.ds(t * STEP, STEP)].reshape(STEP * C, H)
        stage[slot] = dot(lhs, wt[...]).astype(BF16).reshape(STEP, C, stage.shape[3])
        put(t, slot).start()

    for t in range(max(0, laps - slots), laps):
        put(t, t % slots).wait()
    for copy in small:
        copy.wait()


def finish(f, wt, wb, q, k, v):
    R, C, H = f.shape
    W = wt.shape[1]
    laps = R // STEP
    slots = min(4, laps)
    return pl.pallas_call(
        finish_kernel,
        out_shape=(
            jax.ShapeDtypeStruct((R, C, W), BF16),
            jax.ShapeDtypeStruct((H, W), F32),
            jax.ShapeDtypeStruct(q.shape, BF16),
            jax.ShapeDtypeStruct(k.shape, BF16),
            jax.ShapeDtypeStruct(v.shape, BF16),
        ),
        in_specs=[pl.BlockSpec(memory_space=pl.ANY)] + [pl.BlockSpec(memory_space=VMEM)] * 5,
        out_specs=[pl.BlockSpec(memory_space=pl.ANY)] * 5,
        scratch_shapes=[
            VMEM((R, C, H), BF16),
            VMEM((slots, STEP, C, W), BF16),
            VMEM((H, W), F32),
            DMA((laps,)),
            DMA((slots,)),
            DMA((4,)),
        ],
        compiler_params=pltpu.CompilerParams(vmem_limit_bytes=67043328),
    )(f, wt, wb, q, k, v)


def on_device(nrow, ncol, pair, w_bias, queries, keys, values, d_out):
    wt = w_bias.T
    f, wb, q, k, v = main(nrow, ncol, wt, pair, queries, keys, values, d_out)
    d_pair, d_wbias, d_queries, d_keys, d_values = finish(f, wt, wb, q, k, v)
    return d_pair, d_wbias.T, d_queries, d_keys, d_values


def solution(mesh):
    return jax.shard_map(
        functools.partial(on_device, mesh.shape["row"], mesh.shape["col"]),
        mesh=mesh,
        in_specs=(
            P("row", "col", None),
            P(),
            P("row", "col"),
            P("col", "row"),
            P("col", "row"),
            P("row", "col"),
        ),
        out_specs=(P("row", "col", None), P(), P("row", "col"), P("col", "row"), P("col", "row")),
        check_vma=False,
    )
```
